512 devices in a mesh: die: 32 (over x, y), ty: 4 (over z_lo), tx: 4 (over z_hi, core).
Axes of the slice: x: 4, y: 8, z: 8 (z_hi: 2, z_lo: 4; z = z_hi * 4 + z_lo), core: 2. Of those that a mesh axis runs over, the one named last changes fastest.
Arguments:
- raster: float32 [32, 1024, 4096], P('die', 'ty', 'tx'), may hold values from -12 to 12
- shift_pick: int32 [32, 4, 4], P('die', 'ty', 'tx'), may hold values from 0 to 7
- offsets: int32 [32, 4, 4, 2], P('die', 'ty', 'tx'), may hold values from -5 to 4
Outputs:
- next_map: float32 [32, 1024, 4096], P('die', 'ty', 'tx')
- prev_map: float32 [32, 1024, 4096], P('die', 'ty', 'tx')
The draws below stay inside these ranges and needn't reach their ends.
All inputs are finite; a program needn't handle non-finite values.
Results may differ from the reference program's by a relative error of at most 0.0003.
Values sent between devices are 32-bit elements; how exact they have to be, the bound alone decides.
A program may use at most 64 MiB of HBM per device.

```python
import jax
import jax.numpy as jnp
from jax import lax

TH = 256
TW = 1024
R = 4
RG = 6
HW = 11
DIES = 32
TILE_ROWS = 4
TILE_COLS = 4
H = 1024
W = 4096


def touch_ends(entries, rng, low, largest):
    longest = entries.shape.index(max(entries.shape))
    spots = []
    for shift in (0, 1):
        where = [jax.random.randint(jax.random.fold_in(rng, axis), (), 0, length) for axis, length in enumerate(entries.shape)]
        where[longest] = (where[longest] + shift) % entries.shape[longest]
        spots.append(tuple(where))
    return entries.at[spots[0]].set(low).at[spots[1]].set(largest)


def shard_levels(rng, extent, split, smallest, top_value):
    level, own = 1.0, jax.random.fold_in(rng, 6)
    for dim, parts in split:
        steps = jnp.exp(jax.random.uniform(jax.random.fold_in(own, dim), (parts,), jnp.float32, smallest / len(split), top_value / len(split)))
        level = level * jnp.repeat(steps, extent[dim] // parts).reshape([-1 if axis == dim else 1 for axis in range(len(extent))])
    return level


def scatter_about(own_key, dims, width, bound, cuts=(), kind=jnp.bfloat16):
    gain = shard_levels(own_key, dims, cuts, -0.22, 0.18) if cuts else 1.0
    drawn = jax.random.normal(own_key, dims, jnp.float32) * width * gain
    return jnp.minimum(jnp.maximum(drawn, -bound), bound).astype(kind)


def setup_inputs(seed: int = 0) -> dict:
    keys = jax.random.split(jax.random.key(seed), 4)
    raster = scatter_about(keys[0], (DIES, H, W), 2.0, 12.0, ((0, 32), (1, 4), (2, 4)), jnp.float32)
    shift_pick = touch_ends(jax.random.randint(keys[1], (DIES, TILE_ROWS, TILE_COLS), 0, 8), jax.random.fold_in(keys[1], 1), 0, 7).astype(jnp.int32)
    offsets = touch_ends(jax.random.randint(keys[2], (DIES, TILE_ROWS, TILE_COLS, 2), -R - 1, R + 1), jax.random.fold_in(keys[2], 1), -R - 1, R).astype(jnp.int32)
    return dict(raster=raster, shift_pick=shift_pick, offsets=offsets)


def gauss_taps(sigma):
    spots = jnp.arange(-RG, RG + 1).astype(jnp.float32)
    raw = jnp.exp(-spots * spots / (2.0 * sigma * sigma))
    return raw / jnp.sum(raw)


def blur_tile(image, sigma):
    taps = gauss_taps(sigma)
    column_sum = taps[0] * image[0:TH, :]
    for shift in range(1, 2 * RG + 1):
        column_sum = column_sum + taps[shift] * image[shift:shift + TH, :]
    total = taps[0] * column_sum[:, 0:TW]
    for shift in range(1, 2 * RG + 1):
        total = total + taps[shift] * column_sum[:, shift:shift + TW]
    return total


def tile_dog(block, row_off, col_off, pick):
    row_start = (row_off + R + 1).astype(jnp.int32)
    col_start = (col_off + R + 1).astype(jnp.int32)
    window = lax.dynamic_slice(block, (row_start, col_start), (TH + 2 * RG + 1, TW + 2 * RG + 1))
    frac_y = (pick % 4).astype(jnp.float32) * 0.25 + 0.125
    frac_x = (pick // 4).astype(jnp.float32) * 0.5 + 0.25
    upper = (1.0 - frac_x) * window[:-1, :-1] + frac_x * window[:-1, 1:]
    lower = (1.0 - frac_x) * window[1:, :-1] + frac_x * window[1:, 1:]
    aligned = (1.0 - frac_y) * upper + frac_y * lower
    return blur_tile(aligned, 1.0) - blur_tile(aligned, 2.0)


def reference(raster, shift_pick, offsets):
    padded = jnp.pad(raster, ((0, 0), (HW, HW), (HW, HW)))

    def one_tile(index):
        die_num = index // (TILE_ROWS * TILE_COLS)
        row_num = (index // TILE_COLS) % TILE_ROWS
        col_num = index % TILE_COLS
        block = lax.dynamic_slice(padded, (die_num, row_num * TH, col_num * TW), (1, TH + 2 * HW, TW + 2 * HW))[0]
        return tile_dog(block, offsets[die_num, row_num, col_num, 0], offsets[die_num, row_num, col_num, 1], shift_pick[die_num, row_num, col_num])

    indices = jnp.arange(DIES * TILE_ROWS * TILE_COLS, dtype=jnp.int32)
    dogs = lax.map(one_tile, indices)
    dogs = dogs.reshape(DIES, TILE_ROWS, TILE_COLS, TH, TW).transpose(0, 1, 3, 2, 4).reshape(DIES, H, W)
    change = dogs[1:] - dogs[:-1]
    zeros = jnp.zeros((1, H, W), dogs.dtype)
    next_map = jnp.concatenate([change, zeros], axis=0)
    prev_map = jnp.concatenate([zeros, change], axis=0)
    return next_map, prev_map
```

```python
import functools
import math

import jax
import jax.numpy as jnp
from jax import lax
from jax.experimental import pallas as pl
from jax.experimental.pallas import tpu as pltpu
from jax.sharding import PartitionSpec as P

MESH = pl.DeviceIdType.MESH
F32, BF16 = jnp.float32, jnp.bfloat16
TH, TW = 256, 1024
RG = 6
PAD = 16
LANE = 128
CENTER, TOP, BOTTOM = (64, 128), (0, 64), (192, 64)
INNER = ((1, 2), (3, 4), (5, 6))
OUTER = (0, 7)


def tap_weights(step, sigma, frac):
    norm = sum(math.exp(-k * k / (2.0 * sigma * sigma)) for k in range(-RG, RG + 1))

    def gauss(k):
        spot = k.astype(F32)
        value = jnp.exp(spot * spot * (-1.0 / (2.0 * sigma * sigma))) * (1.0 / norm)
        return jnp.where(jnp.abs(k) <= RG, value, 0.0)

    return (1.0 - frac) * gauss(step) + frac * gauss(step - 1)


def split(x):
    high = x.astype(BF16)
    return high, (x - high.astype(F32)).astype(BF16)


def product(ah, al, bh, bl):
    dot = functools.partial(jnp.dot, preferred_element_type=F32)
    return dot(ah, bh) + dot(ah, bl) + dot(al, bh)


def row_matrix(rows, row_off, frac_y):
    span = rows + 2 * PAD
    out = lax.broadcasted_iota(jnp.int32, (rows, span), 0)
    step = lax.broadcasted_iota(jnp.int32, (rows, span), 1) - PAD - out - row_off
    return tap_weights(step, 1.0, frac_y), -tap_weights(step, 2.0, frac_y)


def kernel(pick_ref, off_ref, x_ref, next_ref, prev_ref, pf, ph, plo, wh, wl, ych, ycl, yth, ytl, hh, hl, dog, bn, bp,
           load_sem, row_send, row_recv, col_send, col_recv, send_sem, recv_sem):
    die, ty, tx = lax.axis_index("die"), lax.axis_index("ty"), lax.axis_index("tx")
    dies, tys, txs = lax.axis_size("die"), lax.axis_size("ty"), lax.axis_size("tx")
    up, down = lax.rem(die + 1, dies), lax.rem(die + dies - 1, dies)
    has_above, has_below, has_left, has_right = ty > 0, ty < tys - 1, tx > 0, tx < txs - 1

    bar = pltpu.get_barrier_semaphore()
    for target in (up, down):
        pl.semaphore_signal(bar, inc=1, device_id={"die": target}, device_id_type=MESH)
    for there, axis, target in ((has_above, "ty", ty - 1), (has_below, "ty", ty + 1), (has_left, "tx", tx - 1), (has_right, "tx", tx + 1)):
        @pl.when(there)
        def _(axis=axis, target=target):
            pl.semaphore_signal(bar, inc=1, device_id={axis: target}, device_id_type=MESH)

    loads = []
    for i, (first, count) in enumerate(((48, 160), (0, 48), (208, 48))):
        copy = pltpu.make_async_copy(x_ref.at[pl.ds(first, count)], pf.at[pl.ds(PAD + first, count), pl.ds(LANE, TW)], load_sem.at[i])
        copy.start()
        loads.append(copy)

    pick = pick_ref[0, 0, 0]
    row_off, col_off = off_ref[0, 0, 0, 0], off_ref[0, 0, 0, 1]
    frac_y = lax.rem(pick, 4).astype(F32) * 0.25 + 0.125
    frac_x = lax.div(pick, 4).astype(F32) * 0.5 + 0.25

    out = lax.broadcasted_iota(jnp.int32, (3 * LANE, LANE), 1)
    step = lax.broadcasted_iota(jnp.int32, (3 * LANE, LANE), 0) - LANE - out - col_off
    for s, sigma in enumerate((1.0, 2.0)):
        wh[:, s * LANE:(s + 1) * LANE], wl[:, s * LANE:(s + 1) * LANE] = split(tap_weights(step, sigma, frac_x))
    for (yh, yl), (_, rows) in (((ych, ycl), CENTER), ((yth, ytl), TOP)):
        span = rows + 2 * PAD
        for s, m in enumerate(row_matrix(rows, row_off, frac_y)):
            yh[:, s * span:(s + 1) * span], yl[:, s * span:(s + 1) * span] = split(m)

    @pl.when(ty == 0)
    def _():
        pf[0:PAD, LANE:LANE + TW] = jnp.zeros((PAD, TW), F32)

    @pl.when(ty == tys - 1)
    def _():
        pf[PAD + TH:, LANE:LANE + TW] = jnp.zeros((PAD, TW), F32)

    @pl.when(tx == 0)
    def _():
        pf[:, 0:LANE] = jnp.zeros((TH + 2 * PAD, LANE), F32)

    @pl.when(tx == txs - 1)
    def _():
        pf[:, LANE + TW:] = jnp.zeros((TH + 2 * PAD, LANE), F32)

    def convert(r0, r1, c0, c1):
        ph[r0:r1, c0:c1], plo[r0:r1, c0:c1] = split(pf[r0:r1, c0:c1])

    def compute(strip, pair):
        first, rows = strip
        span = rows + 2 * PAD
        for n, j in enumerate(pair):
            lanes = slice(j * LANE, (j + 3) * LANE)
            h = product(ph[first:first + span, lanes], plo[first:first + span, lanes], wh[...], wl[...])
            high, low = split(h)
            for s in range(2):
                where = (slice(s * span, (s + 1) * span), slice(n * LANE, (n + 1) * LANE))
                hh[where], hl[where] = high[:, s * LANE:(s + 1) * LANE], low[:, s * LANE:(s + 1) * LANE]
        yh, yl = (ych, ycl) if rows == CENTER[1] else (yth, ytl)
        d = product(yh[...], yl[...], hh[0:2 * span, :], hl[0:2 * span, :])
        for n, j in enumerate(pair):
            dog[first:first + rows, j * LANE:(j + 1) * LANE] = d[:, n * LANE:(n + 1) * LANE]

    pieces = []

    def send(strip, pair):
        first, rows = strip
        spots = [(pair[0], 2)] if pair[1] == pair[0] + 1 else [(j, 1) for j in pair]
        for j, blocks in spots:
            i = len(pieces)
            where = (pl.ds(first, rows), pl.ds(j * LANE, blocks * LANE))
            copies = []
            for k, (target, landing) in enumerate(((down, bn), (up, bp))):
                copy = pltpu.make_async_remote_copy(src_ref=dog.at[where], dst_ref=landing.at[where], send_sem=send_sem.at[k, i],
                                                    recv_sem=recv_sem.at[k, i], device_id={"die": target}, device_id_type=MESH)
                copy.start()
                copies.append(copy)
            pieces.append((where, copies))

    loads[0].wait()
    convert(64, 224, LANE, LANE + TW)
    compute(CENTER, INNER[0])
    pl.semaphore_wait(bar, 2 + has_above.astype(jnp.int32) + has_below.astype(jnp.int32) + has_left.astype(jnp.int32) + has_right.astype(jnp.int32))
    send(CENTER, INNER[0])

    loads[1].wait()
    loads[2].wait()
    core = pl.ds(LANE, TW)
    to_above = pltpu.make_async_remote_copy(src_ref=pf.at[pl.ds(PAD, PAD), core], dst_ref=pf.at[pl.ds(PAD + TH, PAD), core],
                                            send_sem=row_send.at[0], recv_sem=row_recv.at[0], device_id={"ty": ty - 1}, device_id_type=MESH)
    to_below = pltpu.make_async_remote_copy(src_ref=pf.at[pl.ds(TH, PAD), core], dst_ref=pf.at[pl.ds(0, PAD), core],
                                            send_sem=row_send.at[1], recv_sem=row_recv.at[1], device_id={"ty": ty + 1}, device_id_type=MESH)
    pl.when(has_above)(lambda: to_above.start())
    pl.when(has_below)(lambda: to_below.start())

    for pair in INNER[1:]:
        compute(CENTER, pair)
        send(CENTER, pair)

    pl.when(has_below)(lambda: to_above.wait_recv())
    pl.when(has_above)(lambda: to_below.wait_recv())
    to_left = pltpu.make_async_remote_copy(src_ref=pf.at[:, pl.ds(LANE, LANE)], dst_ref=pf.at[:, pl.ds(LANE + TW, LANE)],
                                           send_sem=col_send.at[0], recv_sem=col_recv.at[0], device_id={"tx": tx - 1}, device_id_type=MESH)
    to_right = pltpu.make_async_remote_copy(src_ref=pf.at[:, pl.ds(TW, LANE)], dst_ref=pf.at[:, pl.ds(0, LANE)],
                                            send_sem=col_send.at[1], recv_sem=col_recv.at[1], device_id={"tx": tx + 1}, device_id_type=MESH)
    pl.when(has_left)(lambda: to_left.start())
    pl.when(has_right)(lambda: to_right.start())

    convert(0, 64, LANE, LANE + TW)
    convert(224, 288, LANE, LANE + TW)
    for strip in (TOP, BOTTOM):
        for pair in INNER:
            compute(strip, pair)
            send(strip, pair)

    pl.when(has_right)(lambda: to_left.wait_recv())
    pl.when(has_left)(lambda: to_right.wait_recv())
    convert(0, 288, 0, LANE)
    convert(0, 288, LANE + TW, 2 * LANE + TW)
    for strip in (CENTER, TOP, BOTTOM):
        compute(strip, OUTER)
        send(strip, OUTER)

    not_last, not_first = die < dies - 1, die > 0
    for where, (from_next, from_prev) in pieces:
        from_next.wait_recv()
        next_ref[where] = jnp.where(not_last, bn[where] - dog[where], 0.0)
        from_prev.wait_recv()
        prev_ref[where] = jnp.where(not_first, dog[where] - bp[where], 0.0)
    for _, copies in pieces:
        for copy in copies:
            copy.wait_send()
    pl.when(has_above)(lambda: to_above.wait_send())
    pl.when(has_below)(lambda: to_below.wait_send())
    pl.when(has_left)(lambda: to_left.wait_send())
    pl.when(has_right)(lambda: to_right.wait_send())


N_PIECES = 3 * len(INNER) + 6


def body(raster, shift_pick, offsets):
    tile = jax.ShapeDtypeStruct((TH, TW), F32)
    wide, high = TW + 2 * LANE, TH + 2 * PAD
    dma = pltpu.SemaphoreType.DMA
    center, edge = CENTER[1] + 2 * PAD, TOP[1] + 2 * PAD
    next_map, prev_map = pl.pallas_call(
        kernel,
        out_shape=[tile, tile],
        in_specs=[pl.BlockSpec(memory_space=pltpu.SMEM), pl.BlockSpec(memory_space=pltpu.SMEM), pl.BlockSpec(memory_space=pltpu.HBM)],
        out_specs=[pl.BlockSpec(memory_space=pltpu.VMEM)] * 2,
        scratch_shapes=[
            pltpu.VMEM((high, wide), F32), pltpu.VMEM((high, wide), BF16), pltpu.VMEM((high, wide), BF16),
            pltpu.VMEM((3 * LANE, 2 * LANE), BF16), pltpu.VMEM((3 * LANE, 2 * LANE), BF16),
            pltpu.VMEM((CENTER[1], 2 * center), BF16), pltpu.VMEM((CENTER[1], 2 * center), BF16),
            pltpu.VMEM((TOP[1], 2 * edge), BF16), pltpu.VMEM((TOP[1], 2 * edge), BF16),
            pltpu.VMEM((2 * center, 2 * LANE), BF16), pltpu.VMEM((2 * center, 2 * LANE), BF16),
            pltpu.VMEM((TH, TW), F32), pltpu.VMEM((TH, TW), F32), pltpu.VMEM((TH, TW), F32),
            dma((3,)), dma((2,)), dma((2,)), dma((2,)), dma((2,)), dma((2, N_PIECES)), dma((2, N_PIECES)),
        ],
        compiler_params=pltpu.CompilerParams(collective_id=0, has_side_effects=True, vmem_limit_bytes=32 * 1024 * 1024),
    )(shift_pick, offsets, raster[0])
    return next_map[None], prev_map[None]


def solution(mesh):
    in_specs = (P("die", "ty", "tx"), P("die", "ty", "tx"), P("die", "ty", "tx", None))
    out_specs = (P("die", "ty", "tx"), P("die", "ty", "tx"))
    return jax.shard_map(body, mesh=mesh, in_specs=in_specs, out_specs=out_specs, check_vma=False)
```

```python
import functools
import math

import jax
import jax.numpy as jnp
from jax import lax
from jax.experimental import pallas as pl
from jax.experimental.pallas import tpu as pltpu
from jax.sharding import PartitionSpec as P

MESH = pl.DeviceIdType.MESH
F32, BF16 = jnp.float32, jnp.bfloat16
TH, TW = 256, 1024
RG = 6
PAD = 16
LANE = 128
CENTER, TOP, BOTTOM = (64, 128), (0, 64), (192, 64)
INNER = ((1, 2), (3, 4), (5, 6))
OUTER = (0, 7)


def tap_weights(step, sigma, frac):
    norm = sum(math.exp(-k * k / (2.0 * sigma * sigma)) for k in range(-RG, RG + 1))

    def gauss(k):
        spot = k.astype(F32)
        value = jnp.exp(spot * spot * (-1.0 / (2.0 * sigma * sigma))) * (1.0 / norm)
        return jnp.where(jnp.abs(k) <= RG, value, 0.0)

    return (1.0 - frac) * gauss(step) + frac * gauss(step - 1)


def split(x):
    high = x.astype(BF16)
    return high, (x - high.astype(F32)).astype(BF16)


def product(ah, al, bh, bl):
    dot = functools.partial(jnp.dot, preferred_element_type=F32)
    return dot(ah, bh) + dot(ah, bl) + dot(al, bh)


def row_matrix(rows, row_off, frac_y):
    span = rows + 2 * PAD
    out = lax.broadcasted_iota(jnp.int32, (rows, span), 0)
    step = lax.broadcasted_iota(jnp.int32, (rows, span), 1) - PAD - out - row_off
    return tap_weights(step, 1.0, frac_y), -tap_weights(step, 2.0, frac_y)


def kernel(pick_ref, off_hbm, x_ref, next_ref, prev_ref, off_ref, pf, ph, plo, wh, wl, ych, ycl, yth, ytl, hh, hl, dog, bn, bp,
           load_sem, row_send, row_recv, col_send, col_recv, send_sem, recv_sem, ready):
    die, ty, tx = lax.axis_index("die"), lax.axis_index("ty"), lax.axis_index("tx")
    dies, tys, txs = lax.axis_size("die"), lax.axis_size("ty"), lax.axis_size("tx")
    has_next, has_prev = die < dies - 1, die > 0
    has_above, has_below, has_left, has_right = ty > 0, ty < tys - 1, tx > 0, tx < txs - 1

    bar = pltpu.get_barrier_semaphore()
    odd = lax.rem(tx, 2) == 1
    beside = ((has_left, tx - 1), (has_right, tx + 1))
    for there, axis, target in ((has_next, "die", die + 1), (has_prev, "die", die - 1), (has_above, "ty", ty - 1), (has_below, "ty", ty + 1)):
        @pl.when(there)
        def _(axis=axis, target=target):
            pl.semaphore_signal(bar, inc=1, device_id={axis: target}, device_id_type=MESH)

    small = pltpu.make_async_copy(off_hbm, off_ref, load_sem.at[3])
    small.start()
    loads = []
    for i, (first, count) in enumerate(((48, 160), (0, 48), (208, 48))):
        copy = pltpu.make_async_copy(x_ref.at[pl.ds(first, count)], pf.at[pl.ds(PAD + first, count), pl.ds(LANE, TW)], load_sem.at[i])
        copy.start()
        loads.append(copy)

    small.wait()
    pick = pick_ref[0, 0, 0]
    row_off, col_off = off_ref[0, 0, 0, 0], off_ref[0, 0, 0, 1]
    frac_y = lax.rem(pick, 4).astype(F32) * 0.25 + 0.125
    frac_x = lax.div(pick, 4).astype(F32) * 0.5 + 0.25

    out = lax.broadcasted_iota(jnp.int32, (3 * LANE, LANE), 1)
    step = lax.broadcasted_iota(jnp.int32, (3 * LANE, LANE), 0) - LANE - out - col_off
    for s, sigma in enumerate((1.0, 2.0)):
        wh[:, s * LANE:(s + 1) * LANE], wl[:, s * LANE:(s + 1) * LANE] = split(tap_weights(step, sigma, frac_x))
    for (yh, yl), (_, rows) in (((ych, ycl), CENTER), ((yth, ytl), TOP)):
        span = rows + 2 * PAD
        for s, m in enumerate(row_matrix(rows, row_off, frac_y)):
            yh[:, s * span:(s + 1) * span], yl[:, s * span:(s + 1) * span] = split(m)

    @pl.when(ty == 0)
    def _():
        pf[0:PAD, LANE:LANE + TW] = jnp.zeros((PAD, TW), F32)

    @pl.when(ty == tys - 1)
    def _():
        pf[PAD + TH:, LANE:LANE + TW] = jnp.zeros((PAD, TW), F32)

    @pl.when(tx == 0)
    def _():
        pf[:, 0:LANE] = jnp.zeros((TH + 2 * PAD, LANE), F32)

    @pl.when(tx == txs - 1)
    def _():
        pf[:, LANE + TW:] = jnp.zeros((TH + 2 * PAD, LANE), F32)

    def convert(r0, r1, c0, c1):
        ph[r0:r1, c0:c1], plo[r0:r1, c0:c1] = split(pf[r0:r1, c0:c1])

    def compute(strip, pair):
        first, rows = strip
        span = rows + 2 * PAD
        for n, j in enumerate(pair):
            lanes = slice(j * LANE, (j + 3) * LANE)
            h = product(ph[first:first + span, lanes], plo[first:first + span, lanes], wh[...], wl[...])
            high, low = split(h)
            for s in range(2):
                where = (slice(s * span, (s + 1) * span), slice(n * LANE, (n + 1) * LANE))
                hh[where], hl[where] = high[:, s * LANE:(s + 1) * LANE], low[:, s * LANE:(s + 1) * LANE]
        yh, yl = (ych, ycl) if rows == CENTER[1] else (yth, ytl)
        d = product(yh[...], yl[...], hh[0:2 * span, :], hl[0:2 * span, :])
        for n, j in enumerate(pair):
            dog[first:first + rows, j * LANE:(j + 1) * LANE] = d[:, n * LANE:(n + 1) * LANE]

    pieces = []

    def send(strip, pair):
        first, rows = strip
        spots = [(pair[0], 2)] if pair[1] == pair[0] + 1 else [(j, 1) for j in pair]
        for j, blocks in spots:
            i = len(pieces)
            where = (pl.ds(first, rows), pl.ds(j * LANE, blocks * LANE))
            copies = []
            for k, (there, target, landing) in enumerate(((has_prev, die - 1, bn), (has_next, die + 1, bp))):
                copy = pltpu.make_async_remote_copy(src_ref=dog.at[where], dst_ref=landing.at[where], send_sem=send_sem.at[k, i],
                                                    recv_sem=recv_sem.at[k, i], device_id={"die": target}, device_id_type=MESH)
                pl.when(there)(copy.start)
                copies.append(copy)
            pieces.append((where, copies))

    loads[0].wait()
    convert(64, 224, LANE, LANE + TW)
    compute(CENTER, INNER[0])
    count = lambda *flags: sum(flag.astype(jnp.int32) for flag in flags)
    tx_count = count(has_left, has_right)
    pl.semaphore_wait(bar, count(has_next, has_prev, has_above, has_below) + jnp.where(odd, 0, tx_count))
    send(CENTER, INNER[0])
    for there, target in beside:
        @pl.when(there & odd)
        def _(target=target):
            pl.semaphore_signal(bar, inc=1, device_id={"tx": target}, device_id_type=MESH)

        @pl.when(there & jnp.logical_not(odd))
        def _(target=target):
            pl.semaphore_signal(ready, inc=1, device_id={"tx": target}, device_id_type=MESH)

    loads[1].wait()
    loads[2].wait()
    core = pl.ds(LANE, TW)
    to_above = pltpu.make_async_remote_copy(src_ref=pf.at[pl.ds(PAD, PAD), core], dst_ref=pf.at[pl.ds(PAD + TH, PAD), core],
                                            send_sem=row_send.at[0], recv_sem=row_recv.at[0], device_id={"ty": ty - 1}, device_id_type=MESH)
    to_below = pltpu.make_async_remote_copy(src_ref=pf.at[pl.ds(TH, PAD), core], dst_ref=pf.at[pl.ds(0, PAD), core],
                                            send_sem=row_send.at[1], recv_sem=row_recv.at[1], device_id={"ty": ty + 1}, device_id_type=MESH)
    pl.when(has_above)(lambda: to_above.start())
    pl.when(has_below)(lambda: to_below.start())

    for pair in INNER[1:]:
        compute(CENTER, pair)
        send(CENTER, pair)

    pl.when(has_below)(lambda: to_above.wait_recv())
    pl.when(has_above)(lambda: to_below.wait_recv())
    to_left = pltpu.make_async_remote_copy(src_ref=pf.at[:, pl.ds(LANE, LANE)], dst_ref=pf.at[:, pl.ds(LANE + TW, LANE)],
                                           send_sem=col_send.at[0], recv_sem=col_recv.at[0], device_id={"tx": tx - 1}, device_id_type=MESH)
    to_right = pltpu.make_async_remote_copy(src_ref=pf.at[:, pl.ds(TW, LANE)], dst_ref=pf.at[:, pl.ds(0, LANE)],
                                            send_sem=col_send.at[1], recv_sem=col_recv.at[1], device_id={"tx": tx + 1}, device_id_type=MESH)
    pl.when(odd)(lambda: pl.semaphore_wait(ready, tx_count))
    pl.when(has_left)(lambda: to_left.start())
    pl.when(has_right)(lambda: to_right.start())

    convert(0, 64, LANE, LANE + TW)
    convert(224, 288, LANE, LANE + TW)
    for strip in (TOP, BOTTOM):
        for pair in INNER:
            compute(strip, pair)
            send(strip, pair)

    pl.when(has_right)(lambda: to_left.wait_recv())
    pl.when(has_left)(lambda: to_right.wait_recv())
    convert(0, 288, 0, LANE)
    convert(0, 288, LANE + TW, 2 * LANE + TW)
    for strip in (CENTER, TOP, BOTTOM):
        compute(strip, OUTER)
        send(strip, OUTER)

    for there, ref in ((has_next, next_ref), (has_prev, prev_ref)):
        @pl.when(jnp.logical_not(there))
        def _(ref=ref):
            ref[...] = jnp.zeros((TH, TW), F32)

    for where, (to_prev, to_next) in pieces:
        @pl.when(has_next)
        def _(where=where, arrival=to_prev):
            arrival.wait_recv()
            next_ref[where] = bn[where] - dog[where]

        @pl.when(has_prev)
        def _(where=where, arrival=to_next):
            arrival.wait_recv()
            prev_ref[where] = dog[where] - bp[where]

    for _, (to_prev, to_next) in pieces:
        pl.when(has_prev)(to_prev.wait_send)
        pl.when(has_next)(to_next.wait_send)
    pl.when(has_above)(lambda: to_above.wait_send())
    pl.when(has_below)(lambda: to_below.wait_send())
    pl.when(has_left)(lambda: to_left.wait_send())
    pl.when(has_right)(lambda: to_right.wait_send())


def flush(next_in, prev_in, next_out, prev_out, sem):
    parts = 4
    copies = []
    for k, (source, target) in enumerate(((next_in, next_out), (prev_in, prev_out))):
        for i in range(parts):
            rows = pl.ds(i * (TH // parts), TH // parts)
            copies.append(pltpu.make_async_copy(source.at[rows], target.at[rows], sem.at[k, i]))
    for copy in copies:
        copy.start()
    for copy in copies:
        copy.wait()


N_PIECES = 3 * len(INNER) + 6


def body(raster, shift_pick, offsets):
    tile = jax.ShapeDtypeStruct((TH, TW), F32)
    wide, high = TW + 2 * LANE, TH + 2 * PAD
    dma = pltpu.SemaphoreType.DMA
    center, edge = CENTER[1] + 2 * PAD, TOP[1] + 2 * PAD
    next_map, prev_map = pl.pallas_call(
        kernel,
        out_shape=[tile, tile],
        in_specs=[pl.BlockSpec(memory_space=pltpu.SMEM)] + [pl.BlockSpec(memory_space=pltpu.HBM)] * 2,
        out_specs=[pl.BlockSpec(memory_space=pltpu.VMEM)] * 2,
        scratch_shapes=[
            pltpu.SMEM((1, 1, 1, 2), jnp.int32),
            pltpu.VMEM((high, wide), F32), pltpu.VMEM((high, wide), BF16), pltpu.VMEM((high, wide), BF16),
            pltpu.VMEM((3 * LANE, 2 * LANE), BF16), pltpu.VMEM((3 * LANE, 2 * LANE), BF16),
            pltpu.VMEM((CENTER[1], 2 * center), BF16), pltpu.VMEM((CENTER[1], 2 * center), BF16),
            pltpu.VMEM((TOP[1], 2 * edge), BF16), pltpu.VMEM((TOP[1], 2 * edge), BF16),
            pltpu.VMEM((2 * center, 2 * LANE), BF16), pltpu.VMEM((2 * center, 2 * LANE), BF16),
            pltpu.VMEM((TH, TW), F32), pltpu.VMEM((TH, TW), F32), pltpu.VMEM((TH, TW), F32),
            dma((4,)), dma((2,)), dma((2,)), dma((2,)), dma((2,)), dma((2, N_PIECES)), dma((2, N_PIECES)), pltpu.SemaphoreType.REGULAR,
        ],
        compiler_params=pltpu.CompilerParams(collective_id=0, has_side_effects=True, vmem_limit_bytes=32 * 1024 * 1024),
    )(shift_pick, *(pltpu.with_memory_space_constraint(x, pltpu.HBM) for x in (offsets, raster[0])))
    maps = pl.pallas_call(
        flush,
        out_shape=[tile, tile],
        in_specs=[pl.BlockSpec(memory_space=pltpu.VMEM)] * 2,
        out_specs=[pl.BlockSpec(memory_space=pltpu.HBM)] * 2,
        scratch_shapes=[dma((2, 4))],
        compiler_params=pltpu.CompilerParams(vmem_limit_bytes=4 * 1024 * 1024),
    )(*(pltpu.with_memory_space_constraint(x, pltpu.VMEM) for x in (next_map, prev_map)))
    return maps[0][None], maps[1][None]


def solution(mesh):
    in_specs = (P("die", "ty", "tx"), P("die", "ty", "tx"), P("die", "ty", "tx", None))
    out_specs = (P("die", "ty", "tx"), P("die", "ty", "tx"))
    return jax.shard_map(body, mesh=mesh, in_specs=in_specs, out_specs=out_specs, check_vma=False)
```

```python
import functools
import math

import jax
import jax.numpy as jnp
from jax import lax
from jax.experimental import pallas as pl
from jax.experimental.pallas import tpu as pltpu
from jax.sharding import PartitionSpec as P

MESH = pl.DeviceIdType.MESH
F32, BF16 = jnp.float32, jnp.bfloat16
TH, TW = 256, 1024
RG = 6
PAD = 16
LANE = 128
ROWS = 64
SPAN = ROWS + 2 * PAD
UPPER, LOWER, TOP, BOTTOM = 64, 128, 0, 192
INNER = ((1, 2), (3, 4), (5, 6))
OUTER = (0, 7)
GROUPS = (((64, 64, 1, 1), (64, 64, 2, 1), (128, 64, 1, 2), (64, 128, 3, 2), (64, 128, 5, 2)),
          ((0, 64, 1, 6), (192, 64, 1, 6)),
          ((0, 256, 0, 1), (0, 256, 7, 1)))
ARRIVALS = ((128, 768), (128, 768), (256, 256))


def start_rank(die, ty, tx):
    late_first = jnp.where((die == 0) & (ty == 0) & (tx == 0), 50, 0)
    return 13 * ty + 50 * lax.div(tx, 2) - 4 * lax.rem(tx, 2) + late_first


def tap_weights(step, sigma, frac):
    norm = sum(math.exp(-k * k / (2.0 * sigma * sigma)) for k in range(-RG, RG + 1))

    def gauss(k):
        spot = k.astype(F32)
        value = jnp.exp(spot * spot * (-1.0 / (2.0 * sigma * sigma))) * (1.0 / norm)
        return jnp.where(jnp.abs(k) <= RG, value, 0.0)

    return (1.0 - frac) * gauss(step) + frac * gauss(step - 1)


def split(x):
    high = x.astype(BF16)
    return high, (x - high.astype(F32)).astype(BF16)


def product(ah, al, bh, bl):
    dot = functools.partial(jnp.dot, preferred_element_type=F32)
    return dot(ah, bh) + dot(ah, bl) + dot(al, bh)


def kernel(pick_ref, off_hbm, x_ref, next_ref, prev_ref, off_ref, pf, ph, plo, wh, wl, yh, yl, hh, hl, dog, bn, bp,
           load_sem, row_send, row_recv, col_send, col_recv, send_sem, recv_sem, ready):
    die, ty, tx = lax.axis_index("die"), lax.axis_index("ty"), lax.axis_index("tx")
    dies, tys, txs = lax.axis_size("die"), lax.axis_size("ty"), lax.axis_size("tx")
    has_next, has_prev = die < dies - 1, die > 0
    bar = pltpu.get_barrier_semaphore()
    for flag, target in ((has_next, die + 1), (has_prev, die - 1)):
        @pl.when(flag)
        def _(target=target):
            pl.semaphore_signal(bar, inc=1, device_id={"die": target}, device_id_type=MESH)

    has_above, has_below, has_left, has_right = ty > 0, ty < tys - 1, tx > 0, tx < txs - 1
    count = lambda flags: sum(flag.astype(jnp.int32) for flag in flags)

    here = start_rank(die, ty, tx)
    sides = (({"ty": ty + 1}, has_below, (die, ty + 1, tx), 1), ({"ty": ty - 1}, has_above, (die, ty - 1, tx), 0),
             ({"tx": tx + 1}, has_right, (die, ty, tx + 1), 3), ({"tx": tx - 1}, has_left, (die, ty, tx - 1), 2))
    follows = [there & (start_rank(*spot) > here) for _, there, spot, _ in sides]
    leads = [there & (start_rank(*spot) < here) for _, there, spot, _ in sides]
    BELOW, ABOVE, RIGHT, LEFT = range(4)

    def await_follower(side):
        pl.when(follows[side])(lambda: pl.semaphore_wait(ready.at[side], 1))

    for (target, _, _, _), flag in zip(sides, follows):
        @pl.when(flag)
        def _(target=target):
            pl.semaphore_signal(bar, inc=1, device_id=target, device_id_type=MESH)

    small = pltpu.make_async_copy(off_hbm, off_ref, load_sem.at[0])
    small.start()
    loads = []
    for i, (first, rows, left, columns) in enumerate(((48, 96, 0, 512), (144, 64, 0, 512), (48, 160, 512, 512), (0, 48, 0, TW), (208, 48, 0, TW))):
        copy = pltpu.make_async_copy(x_ref.at[pl.ds(first, rows), pl.ds(left, columns)],
                                     pf.at[pl.ds(PAD + first, rows), pl.ds(LANE + left, columns)], load_sem.at[min(i + 1, 4)])
        copy.start()
        loads.append(copy)
    edges = pltpu.make_async_copy(x_ref.at[pl.ds(0, 96)], pf.at[pl.ds(PAD, 96), pl.ds(LANE, TW)], load_sem.at[4])

    band = slice(LANE - PAD, 2 * LANE + PAD)
    for w in (wh, wl):
        w[0:LANE - PAD, :] = jnp.zeros((LANE - PAD, 2 * LANE), BF16)
        w[2 * LANE + PAD:, :] = jnp.zeros((LANE - PAD, 2 * LANE), BF16)
    pick = pick_ref[0, 0, 0]
    frac_y = lax.rem(pick, 4).astype(F32) * 0.25 + 0.125
    frac_x = lax.div(pick, 4).astype(F32) * 0.5 + 0.25
    small.wait()
    row_off, col_off = off_ref[0, 0, 0, 0], off_ref[0, 0, 0, 1]
    iota = lambda shape, dim: lax.broadcasted_iota(jnp.int32, shape, dim)
    step = iota((LANE + 2 * PAD, LANE), 0) - PAD - iota((LANE + 2 * PAD, LANE), 1) - col_off
    for s, sigma in enumerate((1.0, 2.0)):
        lanes = slice(s * LANE, (s + 1) * LANE)
        wh[band, lanes], wl[band, lanes] = split(tap_weights(step, sigma, frac_x))
    column = iota((ROWS, 2 * SPAN), 1)
    step = jnp.where(column < SPAN, column, column - SPAN) - PAD - iota((ROWS, 2 * SPAN), 0) - row_off
    yh[...], yl[...] = split(jnp.where(column < SPAN, tap_weights(step, 1.0, frac_y), -tap_weights(step, 2.0, frac_y)))

    def convert(r0, r1, c0, c1):
        ph[r0:r1, c0:c1], plo[r0:r1, c0:c1] = split(pf[r0:r1, c0:c1])

    def compute(first, pair):
        for n, j in enumerate(pair):
            lanes = slice(j * LANE, (j + 3) * LANE)
            h = product(ph[first:first + SPAN, lanes], plo[first:first + SPAN, lanes], wh[...], wl[...])
            high, low = split(h)
            for s in range(2):
                where = (slice(s * SPAN, (s + 1) * SPAN), slice(n * LANE, (n + 1) * LANE))
                hh[where], hl[where] = high[:, s * LANE:(s + 1) * LANE], low[:, s * LANE:(s + 1) * LANE]
        wide = slice(0, len(pair) * LANE)
        d = product(yh[...], yl[...], hh[:, wide], hl[:, wide])
        for n, j in enumerate(pair):
            dog[first:first + ROWS, j * LANE:(j + 1) * LANE] = d[:, n * LANE:(n + 1) * LANE]

    def transfer(k, group, where):
        target, landing = ((die - 1, bn), (die + 1, bp))[k]
        return pltpu.make_async_remote_copy(src_ref=dog.at[where], dst_ref=landing.at[where], send_sem=send_sem.at[k], recv_sem=recv_sem.at[k, group],
                                            device_id={"die": target}, device_id_type=MESH)

    spots = [[(pl.ds(first, rows), pl.ds(left * LANE, blocks * LANE)) for first, rows, left, blocks in group] for group in GROUPS]
    pieces = [[transfer(k, g, where) for k in range(2)] for g, group in enumerate(spots) for where in group]

    def send(i):
        to_prev, to_next = pieces[i]
        pl.when(has_prev)(to_prev.start)
        pl.when(has_next)(to_next.start)

    core = pl.ds(LANE, TW)
    to_above, to_below = (
        pltpu.make_async_remote_copy(src_ref=pf.at[pl.ds(source, PAD), core], dst_ref=pf.at[pl.ds(target, PAD), core], send_sem=row_send.at[i],
                                     recv_sem=row_recv.at[i], device_id={"ty": to}, device_id_type=MESH)
        for i, (source, target, to) in enumerate(((PAD, PAD + TH, ty - 1), (TH, 0, ty + 1))))
    parts = (pl.ds(PAD, TH), pl.ds(0, PAD), pl.ds(PAD + TH, PAD), pl.ds(0, TH + 2 * PAD))
    to_left, to_right = (
        [pltpu.make_async_remote_copy(src_ref=pf.at[rows, pl.ds(source, LANE)], dst_ref=pf.at[rows, pl.ds(target, LANE)], send_sem=col_send.at[i],
                                      recv_sem=col_recv.at[i], device_id={"tx": to}, device_id_type=MESH) for rows in parts]
        for i, (source, target, to) in enumerate(((LANE, LANE + TW, tx - 1), (TW, 0, tx + 1))))

    loads[0].wait()
    convert(64, 160, LANE, LANE + 512)
    compute(UPPER, INNER[0][:1])
    pl.semaphore_wait(bar, count([has_next, has_prev] + leads))
    for (target, _, _, slot), flag in zip(sides, leads):
        @pl.when(flag)
        def _(target=target, slot=slot):
            pl.semaphore_signal(ready.at[slot], inc=1, device_id=target, device_id_type=MESH)

    send(0)
    compute(UPPER, INNER[0][1:])
    send(1)
    loads[1].wait()
    convert(160, 224, LANE, LANE + 512)
    compute(LOWER, INNER[0])
    send(2)
    loads[2].wait()
    edges.wait()
    pl.when(leads[ABOVE])(to_above.start)
    pl.when(leads[BELOW])(to_below.start)
    pl.when(leads[LEFT])(to_left[0].start)
    pl.when(leads[RIGHT])(to_right[0].start)
    convert(64, 224, LANE + 512, LANE + TW)
    for i, pair in enumerate(INNER[1:]):
        compute(UPPER, pair)
        compute(LOWER, pair)
        send(3 + i)
    for side, copy in ((BELOW, to_below), (ABOVE, to_above)):
        await_follower(side)
        pl.when(follows[side])(copy.start)

    @pl.when(ty == 0)
    def _():
        pf[0:PAD, LANE:LANE + TW] = jnp.zeros((PAD, TW), F32)

    @pl.when(ty == tys - 1)
    def _():
        pf[PAD + TH:, LANE:LANE + TW] = jnp.zeros((PAD, TW), F32)

    pl.when(has_below)(to_above.wait_recv)
    pl.when(has_above)(to_below.wait_recv)
    for i in (1, 2):
        pl.when(leads[LEFT])(to_left[i].start)
        pl.when(leads[RIGHT])(to_right[i].start)
    convert(0, 64, LANE, LANE + TW)
    convert(224, 288, LANE, LANE + TW)
    for i, first in enumerate((TOP, BOTTOM)):
        for pair in INNER:
            compute(first, pair)
        send(5 + i)

    for side, copies in ((RIGHT, to_right), (LEFT, to_left)):
        await_follower(side)
        for copy in copies[:3]:
            pl.when(follows[side])(copy.start)

    @pl.when(tx == 0)
    def _():
        pf[:, 0:LANE] = jnp.zeros((TH + 2 * PAD, LANE), F32)

    @pl.when(tx == txs - 1)
    def _():
        pf[:, LANE + TW:] = jnp.zeros((TH + 2 * PAD, LANE), F32)

    pl.when(has_right)(to_left[3].wait_recv)
    pl.when(has_left)(to_right[3].wait_recv)
    convert(0, 288, 0, LANE)
    convert(0, 288, LANE + TW, 2 * LANE + TW)
    for first in (TOP, UPPER, LOWER, BOTTOM):
        compute(first, OUTER)
    send(7)
    send(8)

    for there, ref in ((has_next, next_ref), (has_prev, prev_ref)):
        @pl.when(jnp.logical_not(there))
        def _(ref=ref):
            ref[...] = jnp.zeros((TH, TW), F32)

    for g, (group, (rows, columns)) in enumerate(zip(spots, ARRIVALS)):
        block = (pl.ds(0, rows), pl.ds(0, columns))

        @pl.when(has_next)
        def _(g=g, group=group, block=block):
            transfer(0, g, block).wait_recv()
            for where in group:
                next_ref[where] = bn[where] - dog[where]

        @pl.when(has_prev)
        def _(g=g, group=group, block=block):
            transfer(1, g, block).wait_recv()
            for where in group:
                prev_ref[where] = dog[where] - bp[where]

    tile = (pl.ds(0, TH), pl.ds(0, TW))
    pl.when(has_prev)(transfer(0, 0, tile).wait_send)
    pl.when(has_next)(transfer(1, 0, tile).wait_send)
    pl.when(has_above)(to_above.wait_send)
    pl.when(has_below)(to_below.wait_send)
    pl.when(has_left)(to_left[3].wait_send)
    pl.when(has_right)(to_right[3].wait_send)


def flush(next_in, prev_in, next_out, prev_out, sem):
    copies = [pltpu.make_async_copy(next_in, next_out, sem.at[0]), pltpu.make_async_copy(prev_in, prev_out, sem.at[1])]
    for copy in copies:
        copy.start()
    for copy in copies:
        copy.wait()


def body(raster, shift_pick, offsets):
    tile = jax.ShapeDtypeStruct((TH, TW), F32)
    wide, high = TW + 2 * LANE, TH + 2 * PAD
    dma = pltpu.SemaphoreType.DMA
    next_map, prev_map = pl.pallas_call(
        kernel,
        out_shape=[tile, tile],
        in_specs=[pl.BlockSpec(memory_space=pltpu.SMEM)] + [pl.BlockSpec(memory_space=pltpu.HBM)] * 2,
        out_specs=[pl.BlockSpec(memory_space=pltpu.VMEM)] * 2,
        scratch_shapes=[
            pltpu.SMEM((1, 1, 1, 2), jnp.int32),
            pltpu.VMEM((high, wide), F32), pltpu.VMEM((high, wide), BF16), pltpu.VMEM((high, wide), BF16),
            pltpu.VMEM((3 * LANE, 2 * LANE), BF16), pltpu.VMEM((3 * LANE, 2 * LANE), BF16),
            pltpu.VMEM((ROWS, 2 * SPAN), BF16), pltpu.VMEM((ROWS, 2 * SPAN), BF16),
            pltpu.VMEM((2 * SPAN, 2 * LANE), BF16), pltpu.VMEM((2 * SPAN, 2 * LANE), BF16),
            pltpu.VMEM((TH, TW), F32), pltpu.VMEM((TH, TW), F32), pltpu.VMEM((TH, TW), F32),
            dma((5,)), dma((2,)), dma((2,)), dma((2,)), dma((2,)), dma((2,)), dma((2, 3)), pltpu.SemaphoreType.REGULAR((4,)),
        ],
        compiler_params=pltpu.CompilerParams(collective_id=0, has_side_effects=True, vmem_limit_bytes=32 * 1024 * 1024),
    )(shift_pick, *(pltpu.with_memory_space_constraint(x, pltpu.HBM) for x in (offsets, raster[0])))
    maps = pl.pallas_call(
        flush,
        out_shape=[tile, tile],
        in_specs=[pl.BlockSpec(memory_space=pltpu.VMEM)] * 2,
        out_specs=[pl.BlockSpec(memory_space=pltpu.HBM)] * 2,
        scratch_shapes=[dma((2,))],
        compiler_params=pltpu.CompilerParams(vmem_limit_bytes=4 * 1024 * 1024),
    )(*(pltpu.with_memory_space_constraint(x, pltpu.VMEM) for x in (next_map, prev_map)))
    return maps[0][None], maps[1][None]


def solution(mesh):
    in_specs = (P("die", "ty", "tx"), P("die", "ty", "tx"), P("die", "ty", "tx", None))
    out_specs = (P("die", "ty", "tx"), P("die", "ty", "tx"))
    return jax.shard_map(body, mesh=mesh, in_specs=in_specs, out_specs=out_specs, check_vma=False)
```

```python
import functools
import math

import jax
import jax.numpy as jnp
from jax import lax
from jax.experimental import pallas as pl
from jax.experimental.pallas import tpu as pltpu
from jax.sharding import PartitionSpec as P

MESH = pl.DeviceIdType.MESH
F32, BF16 = jnp.float32, jnp.bfloat16
TH, TW = 256, 1024
RG = 6
PAD = 16
LANE = 128
ROWS = 64
SPAN = ROWS + 2 * PAD
UPPER, LOWER, TOP, BOTTOM = 64, 128, 0, 192
INNER = ((1, 2), (3, 4), (5, 6))
OUTER = (0, 7)
GROUPS = (((64, 64, 1, 1), (64, 64, 2, 1), (128, 64, 1, 2), (64, 128, 3, 2), (64, 128, 5, 2)),
          ((0, 64, 1, 6), (192, 64, 1, 6)),
          ((0, 256, 0, 1), (0, 256, 7, 1)))
ARRIVALS = ((128, 768), (128, 768), (256, 256))


def start_rank(die, ty, tx):
    late_first = jnp.where((die == 0) & (ty == 0) & (tx == 0), 50, 0)
    return 13 * ty + 50 * lax.div(tx, 2) - 4 * lax.rem(tx, 2) + late_first


def tap_weights(step, sigma, frac):
    norm = sum(math.exp(-k * k / (2.0 * sigma * sigma)) for k in range(-RG, RG + 1))

    def gauss(k):
        spot = k.astype(F32)
        value = jnp.exp(spot * spot * (-1.0 / (2.0 * sigma * sigma))) * (1.0 / norm)
        return jnp.where(jnp.abs(k) <= RG, value, 0.0)

    return (1.0 - frac) * gauss(step) + frac * gauss(step - 1)


def split(x):
    high = x.astype(BF16)
    return high, (x - high.astype(F32)).astype(BF16)


def product(ah, al, bh, bl):
    dot = functools.partial(jnp.dot, preferred_element_type=F32)
    return dot(ah, bh) + dot(ah, bl) + dot(al, bh)


def kernel(pick_ref, off_hbm, x_ref, next_ref, prev_ref, off_ref, pf, ph, plo, wh, wl, yh, yl, hh, hl, dog, bn, bp,
           load_sem, row_send, row_recv, col_send, col_recv, send_sem, recv_sem, ready):
    die, ty, tx = lax.axis_index("die"), lax.axis_index("ty"), lax.axis_index("tx")
    dies, tys, txs = lax.axis_size("die"), lax.axis_size("ty"), lax.axis_size("tx")
    has_next, has_prev = die < dies - 1, die > 0
    bar = pltpu.get_barrier_semaphore()
    for flag, target in ((has_next, die + 1), (has_prev, die - 1)):
        @pl.when(flag)
        def _(target=target):
            pl.semaphore_signal(bar, inc=1, device_id={"die": target}, device_id_type=MESH)

    has_above, has_below, has_left, has_right = ty > 0, ty < tys - 1, tx > 0, tx < txs - 1
    count = lambda flags: sum(flag.astype(jnp.int32) for flag in flags)

    here = start_rank(die, ty, tx)
    sides = (({"ty": ty + 1}, has_below, (die, ty + 1, tx), 1), ({"ty": ty - 1}, has_above, (die, ty - 1, tx), 0),
             ({"tx": tx + 1}, has_right, (die, ty, tx + 1), 3), ({"tx": tx - 1}, has_left, (die, ty, tx - 1), 2))
    follows = [there & (start_rank(*spot) > here) for _, there, spot, _ in sides]
    leads = [there & (start_rank(*spot) < here) for _, there, spot, _ in sides]
    BELOW, ABOVE, RIGHT, LEFT = range(4)

    def await_follower(side):
        pl.when(follows[side])(lambda: pl.semaphore_wait(ready.at[side], 1))

    for (target, _, _, _), flag in zip(sides, follows):
        @pl.when(flag)
        def _(target=target):
            pl.semaphore_signal(bar, inc=1, device_id=target, device_id_type=MESH)

    small = pltpu.make_async_copy(off_hbm, off_ref, load_sem.at[0])
    small.start()
    loads = []
    for i, (first, rows, left, columns) in enumerate(((48, 96, 0, 512), (144, 64, 0, 512), (48, 160, 512, 512), (0, 48, 0, TW), (208, 48, 0, TW))):
        copy = pltpu.make_async_copy(x_ref.at[pl.ds(first, rows), pl.ds(left, columns)],
                                     pf.at[pl.ds(PAD + first, rows), pl.ds(LANE + left, columns)], load_sem.at[min(i + 1, 4)])
        copy.start()
        loads.append(copy)
    edges = pltpu.make_async_copy(x_ref.at[pl.ds(0, 96)], pf.at[pl.ds(PAD, 96), pl.ds(LANE, TW)], load_sem.at[4])

    band = slice(LANE - PAD, 2 * LANE + PAD)
    for w in (wh, wl):
        w[0:LANE - PAD, :] = jnp.zeros((LANE - PAD, 2 * LANE), BF16)
        w[2 * LANE + PAD:, :] = jnp.zeros((LANE - PAD, 2 * LANE), BF16)
    pick = pick_ref[0, 0, 0]
    frac_y = lax.rem(pick, 4).astype(F32) * 0.25 + 0.125
    frac_x = lax.div(pick, 4).astype(F32) * 0.5 + 0.25
    small.wait()
    row_off, col_off = off_ref[0, 0, 0, 0], off_ref[0, 0, 0, 1]
    iota = lambda shape, dim: lax.broadcasted_iota(jnp.int32, shape, dim)
    step = iota((LANE + 2 * PAD, LANE), 0) - PAD - iota((LANE + 2 * PAD, LANE), 1) - col_off
    for s, sigma in enumerate((1.0, 2.0)):
        lanes = slice(s * LANE, (s + 1) * LANE)
        wh[band, lanes], wl[band, lanes] = split(tap_weights(step, sigma, frac_x))
    column = iota((ROWS, 2 * SPAN), 1)
    step = jnp.where(column < SPAN, column, column - SPAN) - PAD - iota((ROWS, 2 * SPAN), 0) - row_off
    yh[...], yl[...] = split(jnp.where(column < SPAN, tap_weights(step, 1.0, frac_y), -tap_weights(step, 2.0, frac_y)))

    def convert(r0, r1, c0, c1):
        ph[r0:r1, c0:c1], plo[r0:r1, c0:c1] = split(pf[r0:r1, c0:c1] - level)

    def compute(first, pair):
        for n, j in enumerate(pair):
            lanes = slice(j * LANE, (j + 3) * LANE)
            h = product(ph[first:first + SPAN, lanes], plo[first:first + SPAN, lanes], wh[...], wl[...])
            high, low = split(h)
            for s in range(2):
                where = (slice(s * SPAN, (s + 1) * SPAN), slice(n * LANE, (n + 1) * LANE))
                hh[where], hl[where] = high[:, s * LANE:(s + 1) * LANE], low[:, s * LANE:(s + 1) * LANE]
        wide = slice(0, len(pair) * LANE)
        d = product(yh[...], yl[...], hh[:, wide], hl[:, wide])
        for n, j in enumerate(pair):
            dog[first:first + ROWS, j * LANE:(j + 1) * LANE] = d[:, n * LANE:(n + 1) * LANE]

    def transfer(k, group, where):
        target, landing = ((die - 1, bn), (die + 1, bp))[k]
        return pltpu.make_async_remote_copy(src_ref=dog.at[where], dst_ref=landing.at[where], send_sem=send_sem.at[k], recv_sem=recv_sem.at[k, group],
                                            device_id={"die": target}, device_id_type=MESH)

    spots = [[(pl.ds(first, rows), pl.ds(left * LANE, blocks * LANE)) for first, rows, left, blocks in group] for group in GROUPS]
    pieces = [[transfer(k, g, where) for k in range(2)] for g, group in enumerate(spots) for where in group]

    def send(i):
        to_prev, to_next = pieces[i]
        pl.when(has_prev)(to_prev.start)
        pl.when(has_next)(to_next.start)

    core = pl.ds(LANE, TW)
    to_above, to_below = (
        pltpu.make_async_remote_copy(src_ref=pf.at[pl.ds(source, PAD), core], dst_ref=pf.at[pl.ds(target, PAD), core], send_sem=row_send.at[i],
                                     recv_sem=row_recv.at[i], device_id={"ty": to}, device_id_type=MESH)
        for i, (source, target, to) in enumerate(((PAD, PAD + TH, ty - 1), (TH, 0, ty + 1))))
    parts = (pl.ds(PAD, TH), pl.ds(0, PAD), pl.ds(PAD + TH, PAD), pl.ds(0, TH + 2 * PAD))
    to_left, to_right = (
        [pltpu.make_async_remote_copy(src_ref=pf.at[rows, pl.ds(source, LANE)], dst_ref=pf.at[rows, pl.ds(target, LANE)], send_sem=col_send.at[i],
                                      recv_sem=col_recv.at[i], device_id={"tx": to}, device_id_type=MESH) for rows in parts]
        for i, (source, target, to) in enumerate(((LANE, LANE + TW, tx - 1), (TW, 0, tx + 1))))

    loads[0].wait()
    level = jnp.mean(pf[64:72, LANE:2 * LANE])
    convert(64, 160, LANE, LANE + 512)
    compute(UPPER, INNER[0][:1])
    pl.semaphore_wait(bar, count([has_next, has_prev] + leads))
    for (target, _, _, slot), flag in zip(sides, leads):
        @pl.when(flag)
        def _(target=target, slot=slot):
            pl.semaphore_signal(ready.at[slot], inc=1, device_id=target, device_id_type=MESH)

    send(0)
    compute(UPPER, INNER[0][1:])
    send(1)
    loads[1].wait()
    convert(160, 224, LANE, LANE + 512)
    compute(LOWER, INNER[0])
    send(2)
    loads[2].wait()
    edges.wait()
    pl.when(leads[ABOVE])(to_above.start)
    pl.when(leads[BELOW])(to_below.start)
    pl.when(leads[LEFT])(to_left[0].start)
    pl.when(leads[RIGHT])(to_right[0].start)
    convert(64, 224, LANE + 512, LANE + TW)
    for i, pair in enumerate(INNER[1:]):
        compute(UPPER, pair)
        compute(LOWER, pair)
        send(3 + i)
    for side, copy in ((BELOW, to_below), (ABOVE, to_above)):
        await_follower(side)
        pl.when(follows[side])(copy.start)

    @pl.when(ty == 0)
    def _():
        pf[0:PAD, LANE:LANE + TW] = jnp.zeros((PAD, TW), F32)

    @pl.when(ty == tys - 1)
    def _():
        pf[PAD + TH:, LANE:LANE + TW] = jnp.zeros((PAD, TW), F32)

    pl.when(has_below)(to_above.wait_recv)
    pl.when(has_above)(to_below.wait_recv)
    for i in (1, 2):
        pl.when(leads[LEFT])(to_left[i].start)
        pl.when(leads[RIGHT])(to_right[i].start)
    convert(0, 64, LANE, LANE + TW)
    convert(224, 288, LANE, LANE + TW)
    for i, first in enumerate((TOP, BOTTOM)):
        for pair in INNER:
            compute(first, pair)
        send(5 + i)

    for side, copies in ((RIGHT, to_right), (LEFT, to_left)):
        await_follower(side)
        for copy in copies[:3]:
            pl.when(follows[side])(copy.start)

    @pl.when(tx == 0)
    def _():
        pf[:, 0:LANE] = jnp.zeros((TH + 2 * PAD, LANE), F32)

    @pl.when(tx == txs - 1)
    def _():
        pf[:, LANE + TW:] = jnp.zeros((TH + 2 * PAD, LANE), F32)

    pl.when(has_right)(to_left[3].wait_recv)
    pl.when(has_left)(to_right[3].wait_recv)
    convert(0, 288, 0, LANE)
    convert(0, 288, LANE + TW, 2 * LANE + TW)
    for first in (TOP, UPPER, LOWER, BOTTOM):
        compute(first, OUTER)
    send(7)
    send(8)

    for there, ref in ((has_next, next_ref), (has_prev, prev_ref)):
        @pl.when(jnp.logical_not(there))
        def _(ref=ref):
            ref[...] = jnp.zeros((TH, TW), F32)

    for g, (group, (rows, columns)) in enumerate(zip(spots, ARRIVALS)):
        block = (pl.ds(0, rows), pl.ds(0, columns))

        @pl.when(has_next)
        def _(g=g, group=group, block=block):
            transfer(0, g, block).wait_recv()
            for where in group:
                next_ref[where] = bn[where] - dog[where]

        @pl.when(has_prev)
        def _(g=g, group=group, block=block):
            transfer(1, g, block).wait_recv()
            for where in group:
                prev_ref[where] = dog[where] - bp[where]

    tile = (pl.ds(0, TH), pl.ds(0, TW))
    pl.when(has_prev)(transfer(0, 0, tile).wait_send)
    pl.when(has_next)(transfer(1, 0, tile).wait_send)
    pl.when(has_above)(to_above.wait_send)
    pl.when(has_below)(to_below.wait_send)
    pl.when(has_left)(to_left[3].wait_send)
    pl.when(has_right)(to_right[3].wait_send)


def flush(next_in, prev_in, next_out, prev_out, sem):
    copies = [pltpu.make_async_copy(next_in, next_out, sem.at[0]), pltpu.make_async_copy(prev_in, prev_out, sem.at[1])]
    for copy in copies:
        copy.start()
    for copy in copies:
        copy.wait()


def body(raster, shift_pick, offsets):
    tile = jax.ShapeDtypeStruct((TH, TW), F32)
    wide, high = TW + 2 * LANE, TH + 2 * PAD
    dma = pltpu.SemaphoreType.DMA
    next_map, prev_map = pl.pallas_call(
        kernel,
        out_shape=[tile, tile],
        in_specs=[pl.BlockSpec(memory_space=pltpu.SMEM)] + [pl.BlockSpec(memory_space=pltpu.HBM)] * 2,
        out_specs=[pl.BlockSpec(memory_space=pltpu.VMEM)] * 2,
        scratch_shapes=[
            pltpu.SMEM((1, 1, 1, 2), jnp.int32),
            pltpu.VMEM((high, wide), F32), pltpu.VMEM((high, wide), BF16), pltpu.VMEM((high, wide), BF16),
            pltpu.VMEM((3 * LANE, 2 * LANE), BF16), pltpu.VMEM((3 * LANE, 2 * LANE), BF16),
            pltpu.VMEM((ROWS, 2 * SPAN), BF16), pltpu.VMEM((ROWS, 2 * SPAN), BF16),
            pltpu.VMEM((2 * SPAN, 2 * LANE), BF16), pltpu.VMEM((2 * SPAN, 2 * LANE), BF16),
            pltpu.VMEM((TH, TW), F32), pltpu.VMEM((TH, TW), F32), pltpu.VMEM((TH, TW), F32),
            dma((5,)), dma((2,)), dma((2,)), dma((2,)), dma((2,)), dma((2,)), dma((2, 3)), pltpu.SemaphoreType.REGULAR((4,)),
        ],
        compiler_params=pltpu.CompilerParams(collective_id=0, has_side_effects=True, vmem_limit_bytes=32 * 1024 * 1024),
    )(shift_pick, *(pltpu.with_memory_space_constraint(x, pltpu.HBM) for x in (offsets, raster[0])))
    maps = pl.pallas_call(
        flush,
        out_shape=[tile, tile],
        in_specs=[pl.BlockSpec(memory_space=pltpu.VMEM)] * 2,
        out_specs=[pl.BlockSpec(memory_space=pltpu.HBM)] * 2,
        scratch_shapes=[dma((2,))],
        compiler_params=pltpu.CompilerParams(vmem_limit_bytes=4 * 1024 * 1024),
    )(*(pltpu.with_memory_space_constraint(x, pltpu.VMEM) for x in (next_map, prev_map)))
    return maps[0][None], maps[1][None]


def solution(mesh):
    in_specs = (P("die", "ty", "tx"), P("die", "ty", "tx"), P("die", "ty", "tx", None))
    out_specs = (P("die", "ty", "tx"), P("die", "ty", "tx"))
    return jax.shard_map(body, mesh=mesh, in_specs=in_specs, out_specs=out_specs, check_vma=False)
```

```python
import functools
import math

import jax
import jax.numpy as jnp
from jax import lax
from jax.experimental import pallas as pl
from jax.experimental.pallas import tpu as pltpu
from jax.sharding import PartitionSpec as P

MESH = pl.DeviceIdType.MESH
F32, BF16 = jnp.float32, jnp.bfloat16
TH, TW = 256, 1024
RG = 6
PAD = 16
LANE = 128
ROWS = 64
SPAN = ROWS + 2 * PAD
UPPER, LOWER, TOP, BOTTOM = 64, 128, 0, 192
INNER = ((1, 2), (3, 4), (5, 6))
OUTER = (0, 7)
GROUPS = (((64, 64, 1, 1), (64, 64, 2, 1), (128, 64, 1, 2), (64, 128, 3, 2), (64, 128, 5, 2)),
          ((0, 64, 1, 6), (192, 64, 1, 6)),
          ((0, 256, 0, 1), (0, 256, 7, 1)))
ARRIVALS = ((128, 768), (128, 768), (256, 256))


def start_rank(die, ty, tx):
    late_first = jnp.where((die == 0) & (ty == 0) & (tx == 0), 50, 0)
    return 13 * ty + 50 * lax.div(tx, 2) - 4 * lax.rem(tx, 2) + late_first


def tap_weights(step, sigma, frac):
    norm = sum(math.exp(-k * k / (2.0 * sigma * sigma)) for k in range(-RG, RG + 1))

    def gauss(k):
        spot = k.astype(F32)
        value = jnp.exp(spot * spot * (-1.0 / (2.0 * sigma * sigma))) * (1.0 / norm)
        return jnp.where(jnp.abs(k) <= RG, value, 0.0)

    return (1.0 - frac) * gauss(step) + frac * gauss(step - 1)


def split(x):
    high = x.astype(BF16)
    return high, (x - high.astype(F32)).astype(BF16)


def product(ah, al, bh, bl):
    dot = functools.partial(jnp.dot, preferred_element_type=F32)
    return dot(ah, bh) + dot(ah, bl) + dot(al, bh)


def kernel(pick_ref, off_hbm, x_ref, next_ref, prev_ref, off_ref, pf, wh, wl, yh, yl, hh, hl, dog, bn, bp,
           load_sem, row_send, row_recv, col_send, col_recv, send_sem, recv_sem, ready):
    die, ty, tx = lax.axis_index("die"), lax.axis_index("ty"), lax.axis_index("tx")
    dies, tys, txs = lax.axis_size("die"), lax.axis_size("ty"), lax.axis_size("tx")
    has_next, has_prev = die < dies - 1, die > 0
    bar = pltpu.get_barrier_semaphore()
    for flag, target in ((has_next, die + 1), (has_prev, die - 1)):
        @pl.when(flag)
        def _(target=target):
            pl.semaphore_signal(bar, inc=1, device_id={"die": target}, device_id_type=MESH)

    def load(i, first, rows, left, columns):
        return pltpu.make_async_copy(x_ref.at[pl.ds(first, rows), pl.ds(left, columns)],
                                     pf.at[pl.ds(PAD + first, rows), pl.ds(LANE + left, columns)], load_sem.at[i])

    small = pltpu.make_async_copy(off_hbm, off_ref, load_sem.at[0])
    loads = (load(1, 48, 96, 0, 512), load(2, 144, 64, 0, 512), load(3, 48, 160, 512, 512), load(4, 0, 96, 0, TW))
    small.start()
    for first in (48, 80, 112):
        load(1, first, 32, 0, 512).start()
    for copy in (loads[1], loads[2], load(4, 0, 48, 0, TW), load(4, 208, 48, 0, TW)):
        copy.start()

    has_above, has_below, has_left, has_right = ty > 0, ty < tys - 1, tx > 0, tx < txs - 1
    count = lambda flags: sum(flag.astype(jnp.int32) for flag in flags)

    here = start_rank(die, ty, tx)
    sides = (({"ty": ty + 1}, has_below, (die, ty + 1, tx), 1), ({"ty": ty - 1}, has_above, (die, ty - 1, tx), 0),
             ({"tx": tx + 1}, has_right, (die, ty, tx + 1), 3), ({"tx": tx - 1}, has_left, (die, ty, tx - 1), 2))
    follows = [there & (start_rank(*spot) > here) for _, there, spot, _ in sides]
    leads = [there & (start_rank(*spot) < here) for _, there, spot, _ in sides]
    BELOW, ABOVE, RIGHT, LEFT = range(4)

    def await_follower(side):
        pl.when(follows[side])(lambda: pl.semaphore_wait(ready.at[side], 1))

    for (target, _, _, _), flag in zip(sides, follows):
        @pl.when(flag)
        def _(target=target):
            pl.semaphore_signal(bar, inc=1, device_id=target, device_id_type=MESH)

    band = slice(LANE - PAD, 2 * LANE + PAD)
    for w in (wh, wl):
        w[0:LANE - PAD, :] = jnp.zeros((LANE - PAD, 2 * LANE), BF16)
        w[2 * LANE + PAD:, :] = jnp.zeros((LANE - PAD, 2 * LANE), BF16)
    pick = pick_ref[0, 0, 0]
    frac_y = lax.rem(pick, 4).astype(F32) * 0.25 + 0.125
    frac_x = lax.div(pick, 4).astype(F32) * 0.5 + 0.25
    small.wait()
    row_off, col_off = off_ref[0, 0, 0, 0], off_ref[0, 0, 0, 1]
    iota = lambda shape, dim: lax.broadcasted_iota(jnp.int32, shape, dim)
    step = iota((LANE + 2 * PAD, LANE), 0) - PAD - iota((LANE + 2 * PAD, LANE), 1) - col_off
    for s, sigma in enumerate((1.0, 2.0)):
        lanes = slice(s * LANE, (s + 1) * LANE)
        wh[band, lanes], wl[band, lanes] = split(tap_weights(step, sigma, frac_x))
    column = iota((ROWS, 2 * SPAN), 1)
    step = jnp.where(column < SPAN, column, column - SPAN) - PAD - iota((ROWS, 2 * SPAN), 0) - row_off
    yh[...], yl[...] = split(jnp.where(column < SPAN, tap_weights(step, 1.0, frac_y), -tap_weights(step, 2.0, frac_y)))

    def compute(first, pair):
        level = jnp.mean(pf[first + 40:first + 48, (pair[0] + 1) * LANE:(pair[0] + 2) * LANE], keepdims=True)
        for n, j in enumerate(pair):
            if pair == OUTER and n == 1:
                level = jnp.mean(pf[first + 40:first + 48, (j + 1) * LANE:(j + 2) * LANE], keepdims=True)
            high, low = split(product(*split(pf[first:first + SPAN, j * LANE:(j + 3) * LANE] - level), wh[...], wl[...]))
            for s in range(2):
                where = (slice(s * SPAN, (s + 1) * SPAN), slice(n * LANE, (n + 1) * LANE))
                hh[where], hl[where] = high[:, s * LANE:(s + 1) * LANE], low[:, s * LANE:(s + 1) * LANE]
        wide = slice(0, len(pair) * LANE)
        d = product(yh[...], yl[...], hh[:, wide], hl[:, wide])
        for n, j in enumerate(pair):
            dog[first:first + ROWS, j * LANE:(j + 1) * LANE] = d[:, n * LANE:(n + 1) * LANE]

    def transfer(k, group, where):
        target, landing = ((die - 1, bn), (die + 1, bp))[k]
        return pltpu.make_async_remote_copy(src_ref=dog.at[where], dst_ref=landing.at[where], send_sem=send_sem.at[k], recv_sem=recv_sem.at[k, group],
                                            device_id={"die": target}, device_id_type=MESH)

    spots = [[(pl.ds(first, rows), pl.ds(left * LANE, blocks * LANE)) for first, rows, left, blocks in group] for group in GROUPS]
    pieces = [[transfer(k, g, where) for k in range(2)] for g, group in enumerate(spots) for where in group]

    def send(i):
        to_prev, to_next = pieces[i]
        pl.when(has_prev)(to_prev.start)
        pl.when(has_next)(to_next.start)

    core = pl.ds(LANE, TW)
    to_above, to_below = (
        pltpu.make_async_remote_copy(src_ref=pf.at[pl.ds(source, PAD), core], dst_ref=pf.at[pl.ds(target, PAD), core], send_sem=row_send.at[i],
                                     recv_sem=row_recv.at[i], device_id={"ty": to}, device_id_type=MESH)
        for i, (source, target, to) in enumerate(((PAD, PAD + TH, ty - 1), (TH, 0, ty + 1))))
    parts = (pl.ds(PAD, TH), pl.ds(0, PAD), pl.ds(PAD + TH, PAD), pl.ds(0, TH + 2 * PAD))
    to_left, to_right = (
        [pltpu.make_async_remote_copy(src_ref=pf.at[rows, pl.ds(source, LANE)], dst_ref=pf.at[rows, pl.ds(target, LANE)], send_sem=col_send.at[i],
                                      recv_sem=col_recv.at[i], device_id={"tx": to}, device_id_type=MESH) for rows in parts]
        for i, (source, target, to) in enumerate(((LANE, LANE + TW, tx - 1), (TW, 0, tx + 1))))

    loads[0].wait()
    compute(UPPER, INNER[0][:1])
    pl.semaphore_wait(bar, count([has_next, has_prev] + leads))
    for (target, _, _, slot), flag in zip(sides, leads):
        @pl.when(flag)
        def _(target=target, slot=slot):
            pl.semaphore_signal(ready.at[slot], inc=1, device_id=target, device_id_type=MESH)

    send(0)
    compute(UPPER, INNER[0][1:])
    send(1)
    loads[1].wait()
    compute(LOWER, INNER[0])
    send(2)
    loads[2].wait()
    loads[3].wait()
    pl.when(leads[ABOVE])(to_above.start)
    pl.when(leads[BELOW])(to_below.start)
    pl.when(leads[LEFT])(to_left[0].start)
    pl.when(leads[RIGHT])(to_right[0].start)
    for i, pair in enumerate(INNER[1:]):
        compute(UPPER, pair)
        compute(LOWER, pair)
        send(3 + i)
    for side, copy in ((BELOW, to_below), (ABOVE, to_above)):
        await_follower(side)
        pl.when(follows[side])(copy.start)

    @pl.when(ty == 0)
    def _():
        pf[0:PAD, LANE:LANE + TW] = jnp.zeros((PAD, TW), F32)

    @pl.when(ty == tys - 1)
    def _():
        pf[PAD + TH:, LANE:LANE + TW] = jnp.zeros((PAD, TW), F32)

    pl.when(has_below)(to_above.wait_recv)
    pl.when(has_above)(to_below.wait_recv)
    for i in (1, 2):
        pl.when(leads[LEFT])(to_left[i].start)
        pl.when(leads[RIGHT])(to_right[i].start)
    for i, first in enumerate((TOP, BOTTOM)):
        for pair in INNER:
            compute(first, pair)
        send(5 + i)

    for side, copies in ((RIGHT, to_right), (LEFT, to_left)):
        await_follower(side)
        for copy in copies[:3]:
            pl.when(follows[side])(copy.start)

    @pl.when(tx == 0)
    def _():
        pf[:, 0:LANE] = jnp.zeros((TH + 2 * PAD, LANE), F32)

    @pl.when(tx == txs - 1)
    def _():
        pf[:, LANE + TW:] = jnp.zeros((TH + 2 * PAD, LANE), F32)

    pl.when(has_right)(to_left[3].wait_recv)
    pl.when(has_left)(to_right[3].wait_recv)
    for first in (TOP, UPPER, LOWER, BOTTOM):
        compute(first, OUTER)
    send(7)
    send(8)

    for there, ref in ((has_next, next_ref), (has_prev, prev_ref)):
        @pl.when(jnp.logical_not(there))
        def _(ref=ref):
            ref[...] = jnp.zeros((TH, TW), F32)

    for g, (group, (rows, columns)) in enumerate(zip(spots, ARRIVALS)):
        block = (pl.ds(0, rows), pl.ds(0, columns))

        @pl.when(has_next)
        def _(g=g, group=group, block=block):
            transfer(0, g, block).wait_recv()
            for where in group:
                next_ref[where] = bn[where] - dog[where]

        @pl.when(has_prev)
        def _(g=g, group=group, block=block):
            transfer(1, g, block).wait_recv()
            for where in group:
                prev_ref[where] = dog[where] - bp[where]

    tile = (pl.ds(0, TH), pl.ds(0, TW))
    pl.when(has_prev)(transfer(0, 0, tile).wait_send)
    pl.when(has_next)(transfer(1, 0, tile).wait_send)
    pl.when(has_above)(to_above.wait_send)
    pl.when(has_below)(to_below.wait_send)
    pl.when(has_left)(to_left[3].wait_send)
    pl.when(has_right)(to_right[3].wait_send)


def flush(next_in, prev_in, next_out, prev_out, sem):
    copies = [pltpu.make_async_copy(next_in, next_out, sem.at[0]), pltpu.make_async_copy(prev_in, prev_out, sem.at[1])]
    for copy in copies:
        copy.start()
    for copy in copies:
        copy.wait()


def body(raster, shift_pick, offsets):
    tile = jax.ShapeDtypeStruct((TH, TW), F32)
    wide, high = TW + 2 * LANE, TH + 2 * PAD
    dma = pltpu.SemaphoreType.DMA
    next_map, prev_map = pl.pallas_call(
        kernel,
        out_shape=[tile, tile],
        in_specs=[pl.BlockSpec(memory_space=pltpu.SMEM)] + [pl.BlockSpec(memory_space=pltpu.HBM)] * 2,
        out_specs=[pl.BlockSpec(memory_space=pltpu.VMEM)] * 2,
        scratch_shapes=[
            pltpu.SMEM((1, 1, 1, 2), jnp.int32),
            pltpu.VMEM((high, wide), F32),
            pltpu.VMEM((3 * LANE, 2 * LANE), BF16), pltpu.VMEM((3 * LANE, 2 * LANE), BF16),
            pltpu.VMEM((ROWS, 2 * SPAN), BF16), pltpu.VMEM((ROWS, 2 * SPAN), BF16),
            pltpu.VMEM((2 * SPAN, 2 * LANE), BF16), pltpu.VMEM((2 * SPAN, 2 * LANE), BF16),
            pltpu.VMEM((TH, TW), F32), pltpu.VMEM((TH, TW), F32), pltpu.VMEM((TH, TW), F32),
            dma((5,)), dma((2,)), dma((2,)), dma((2,)), dma((2,)), dma((2,)), dma((2, 3)), pltpu.SemaphoreType.REGULAR((4,)),
        ],
        compiler_params=pltpu.CompilerParams(collective_id=0, has_side_effects=True, vmem_limit_bytes=32 * 1024 * 1024),
    )(shift_pick, *(pltpu.with_memory_space_constraint(x, pltpu.HBM) for x in (offsets, raster[0])))
    maps = pl.pallas_call(
        flush,
        out_shape=[tile, tile],
        in_specs=[pl.BlockSpec(memory_space=pltpu.VMEM)] * 2,
        out_specs=[pl.BlockSpec(memory_space=pltpu.HBM)] * 2,
        scratch_shapes=[dma((2,))],
        compiler_params=pltpu.CompilerParams(vmem_limit_bytes=4 * 1024 * 1024),
    )(*(pltpu.with_memory_space_constraint(x, pltpu.VMEM) for x in (next_map, prev_map)))
    return maps[0][None], maps[1][None]


def solution(mesh):
    in_specs = (P("die", "ty", "tx"), P("die", "ty", "tx"), P("die", "ty", "tx", None))
    out_specs = (P("die", "ty", "tx"), P("die", "ty", "tx"))
    return jax.shard_map(body, mesh=mesh, in_specs=in_specs, out_specs=out_specs, check_vma=False)
```

```python
import functools
import math

import jax
import jax.numpy as jnp
from jax import lax
from jax.experimental import pallas as pl
from jax.experimental.pallas import tpu as pltpu
from jax.sharding import PartitionSpec as P

MESH = pl.DeviceIdType.MESH
F32, BF16 = jnp.float32, jnp.bfloat16
TH, TW = 256, 1024
RG = 6
PAD = 16
LANE = 128
ROWS = 64
SPAN = ROWS + 2 * PAD
UPPER, LOWER, TOP, BOTTOM = 64, 128, 0, 192
INNER = ((1, 2), (3, 4), (5, 6))
OUTER = (0, 7)
GROUPS = (((64, 64, 1, 1), (64, 64, 2, 1), (128, 64, 1, 2), (64, 128, 3, 2), (64, 128, 5, 2)),
          ((0, 64, 1, 6), (192, 64, 1, 6)),
          ((0, 256, 0, 1), (0, 256, 7, 1)))
ARRIVALS = ((6, 128), (6, 128), (2, 256))


def start_rank(die, ty, tx):
    late_first = jnp.where((die == 0) & (ty == 0) & (tx == 0), 50, 0)
    return 13 * ty + 50 * lax.div(tx, 2) - 4 * lax.rem(tx, 2) + late_first


def tap_weights(step, sigma, frac):
    norm = sum(math.exp(-k * k / (2.0 * sigma * sigma)) for k in range(-RG, RG + 1))

    def gauss(k):
        spot = k.astype(F32)
        value = jnp.exp(spot * spot * (-1.0 / (2.0 * sigma * sigma))) * (1.0 / norm)
        return jnp.where(jnp.abs(k) <= RG, value, 0.0)

    return (1.0 - frac) * gauss(step) + frac * gauss(step - 1)


def split(x):
    high = x.astype(BF16)
    return high, (x - high.astype(F32)).astype(BF16)


def product(ah, al, bh, bl):
    dot = functools.partial(jnp.dot, preferred_element_type=F32)
    return dot(ah, bh) + dot(ah, bl) + dot(al, bh)


def kernel(pick_ref, off_hbm, x_ref, next_ref, prev_ref, off_ref, pf, wh, wl, yh, yl, hh, hl, dog, bn, bp,
           load_sem, row_send, row_recv, col_send, col_recv, send_sem, recv_sem, ready):
    die, ty, tx = lax.axis_index("die"), lax.axis_index("ty"), lax.axis_index("tx")
    dies, tys, txs = lax.axis_size("die"), lax.axis_size("ty"), lax.axis_size("tx")
    has_next, has_prev = die < dies - 1, die > 0
    bar = pltpu.get_barrier_semaphore()
    for flag, target in ((has_next, die + 1), (has_prev, die - 1)):
        @pl.when(flag)
        def _(target=target):
            pl.semaphore_signal(bar, inc=1, device_id={"die": target}, device_id_type=MESH)

    def load(i, first, rows, left, columns):
        return pltpu.make_async_copy(x_ref.at[pl.ds(first, rows), pl.ds(left, columns)],
                                     pf.at[pl.ds(PAD + first, rows), pl.ds(LANE + left, columns)], load_sem.at[i])

    small = pltpu.make_async_copy(off_hbm, off_ref, load_sem.at[0])
    loads = (load(1, 48, 96, 0, 512), load(2, 0, 208, 0, TW))
    small.start()
    for first in (48, 80, 112):
        load(1, first, 32, 0, 512).start()
    for copy in (load(2, 144, 64, 0, 512), load(2, 48, 160, 512, 512), load(2, 0, 48, 0, TW), load(2, 208, 48, 0, TW)):
        copy.start()

    has_above, has_below, has_left, has_right = ty > 0, ty < tys - 1, tx > 0, tx < txs - 1
    count = lambda flags: sum(flag.astype(jnp.int32) for flag in flags)

    here = start_rank(die, ty, tx)
    sides = (({"ty": ty + 1}, has_below, (die, ty + 1, tx), 1), ({"ty": ty - 1}, has_above, (die, ty - 1, tx), 0),
             ({"tx": tx + 1}, has_right, (die, ty, tx + 1), 3), ({"tx": tx - 1}, has_left, (die, ty, tx - 1), 2))
    follows = [there & (start_rank(*spot) > here) for _, there, spot, _ in sides]
    leads = [there & (start_rank(*spot) < here) for _, there, spot, _ in sides]
    BELOW, ABOVE, RIGHT, LEFT = range(4)

    def await_follower(side):
        pl.when(follows[side])(lambda: pl.semaphore_wait(ready.at[side], 1))

    for (target, _, _, _), flag in zip(sides, follows):
        @pl.when(flag)
        def _(target=target):
            pl.semaphore_signal(bar, inc=1, device_id=target, device_id_type=MESH)

    band = slice(LANE - PAD, 2 * LANE + PAD)
    for w in (wh, wl):
        w[0:LANE - PAD, :] = jnp.zeros((LANE - PAD, 2 * LANE), BF16)
        w[2 * LANE + PAD:, :] = jnp.zeros((LANE - PAD, 2 * LANE), BF16)
    pick = pick_ref[0, 0, 0]
    frac_y = lax.rem(pick, 4).astype(F32) * 0.25 + 0.125
    frac_x = lax.div(pick, 4).astype(F32) * 0.5 + 0.25
    small.wait()
    row_off, col_off = off_ref[0, 0, 0, 0], off_ref[0, 0, 0, 1]
    iota = lambda shape, dim: lax.broadcasted_iota(jnp.int32, shape, dim)
    step = iota((LANE + 2 * PAD, LANE), 0) - PAD - iota((LANE + 2 * PAD, LANE), 1) - col_off
    for s, sigma in enumerate((1.0, 2.0)):
        lanes = slice(s * LANE, (s + 1) * LANE)
        wh[band, lanes], wl[band, lanes] = split(tap_weights(step, sigma, frac_x))
    column = iota((ROWS, 2 * SPAN), 1)
    step = jnp.where(column < SPAN, column, column - SPAN) - PAD - iota((ROWS, 2 * SPAN), 0) - row_off
    yh[...], yl[...] = split(jnp.where(column < SPAN, tap_weights(step, 1.0, frac_y), -tap_weights(step, 2.0, frac_y)))

    def compute(first, pair):
        level = jnp.mean(pf[first + 40:first + 48, (pair[0] + 1) * LANE:(pair[0] + 2) * LANE], keepdims=True)
        for n, j in enumerate(pair):
            if pair == OUTER and n == 1:
                level = jnp.mean(pf[first + 40:first + 48, (j + 1) * LANE:(j + 2) * LANE], keepdims=True)
            high, low = split(product(*split(pf[first:first + SPAN, j * LANE:(j + 3) * LANE] - level), wh[...], wl[...]))
            for s in range(2):
                where = (slice(s * SPAN, (s + 1) * SPAN), slice(n * LANE, (n + 1) * LANE))
                hh[where], hl[where] = high[:, s * LANE:(s + 1) * LANE], low[:, s * LANE:(s + 1) * LANE]
        wide = slice(0, len(pair) * LANE)
        d = product(yh[...], yl[...], hh[:, wide], hl[:, wide])
        for n, j in enumerate(pair):
            dog[j, first:first + ROWS, :] = d[:, n * LANE:(n + 1) * LANE]

    def transfer(k, group, where):
        target, landing = ((die - 1, bn), (die + 1, bp))[k]
        return pltpu.make_async_remote_copy(src_ref=dog.at[where], dst_ref=landing.at[where], send_sem=send_sem.at[k], recv_sem=recv_sem.at[k, group],
                                            device_id={"die": target}, device_id_type=MESH)

    spots = [[(pl.ds(left, blocks), pl.ds(first, rows)) for first, rows, left, blocks in group] for group in GROUPS]
    pieces = [[transfer(k, g, where) for k in range(2)] for g, group in enumerate(spots) for where in group]

    def send(i):
        to_prev, to_next = pieces[i]
        pl.when(has_prev)(to_prev.start)
        pl.when(has_next)(to_next.start)

    core = pl.ds(LANE, TW)
    to_above, to_below = (
        pltpu.make_async_remote_copy(src_ref=pf.at[pl.ds(source, PAD), core], dst_ref=pf.at[pl.ds(target, PAD), core], send_sem=row_send.at[i],
                                     recv_sem=row_recv.at[i], device_id={"ty": to}, device_id_type=MESH)
        for i, (source, target, to) in enumerate(((PAD, PAD + TH, ty - 1), (TH, 0, ty + 1))))
    parts = (pl.ds(PAD, TH), pl.ds(0, PAD), pl.ds(PAD + TH, PAD), pl.ds(0, TH + 2 * PAD))
    to_left, to_right = (
        [pltpu.make_async_remote_copy(src_ref=pf.at[rows, pl.ds(source, LANE)], dst_ref=pf.at[rows, pl.ds(target, LANE)], send_sem=col_send.at[i],
                                      recv_sem=col_recv.at[i], device_id={"tx": to}, device_id_type=MESH) for rows in parts]
        for i, (source, target, to) in enumerate(((LANE, LANE + TW, tx - 1), (TW, 0, tx + 1))))

    loads[0].wait()
    compute(UPPER, INNER[0][:1])
    pl.semaphore_wait(bar, count([has_next, has_prev] + leads))
    for (target, _, _, slot), flag in zip(sides, leads):
        @pl.when(flag)
        def _(target=target, slot=slot):
            pl.semaphore_signal(ready.at[slot], inc=1, device_id=target, device_id_type=MESH)

    send(0)
    compute(UPPER, INNER[0][1:])
    send(1)
    loads[1].wait()
    compute(LOWER, INNER[0])
    send(2)
    pl.when(leads[ABOVE])(to_above.start)
    pl.when(leads[BELOW])(to_below.start)
    pl.when(leads[LEFT])(to_left[0].start)
    pl.when(leads[RIGHT])(to_right[0].start)
    for i, pair in enumerate(INNER[1:]):
        compute(UPPER, pair)
        compute(LOWER, pair)
        send(3 + i)
    for side, copy in ((BELOW, to_below), (ABOVE, to_above)):
        await_follower(side)
        pl.when(follows[side])(copy.start)

    @pl.when(ty == 0)
    def _():
        pf[0:PAD, LANE:LANE + TW] = jnp.zeros((PAD, TW), F32)

    @pl.when(ty == tys - 1)
    def _():
        pf[PAD + TH:, LANE:LANE + TW] = jnp.zeros((PAD, TW), F32)

    pl.when(has_below)(to_above.wait_recv)
    pl.when(has_above)(to_below.wait_recv)
    for i in (1, 2):
        pl.when(leads[LEFT])(to_left[i].start)
        pl.when(leads[RIGHT])(to_right[i].start)
    for i, first in enumerate((TOP, BOTTOM)):
        for pair in INNER:
            compute(first, pair)
        send(5 + i)

    for side, copies in ((RIGHT, to_right), (LEFT, to_left)):
        await_follower(side)
        for copy in copies[:3]:
            pl.when(follows[side])(copy.start)

    @pl.when(tx == 0)
    def _():
        pf[:, 0:LANE] = jnp.zeros((TH + 2 * PAD, LANE), F32)

    @pl.when(tx == txs - 1)
    def _():
        pf[:, LANE + TW:] = jnp.zeros((TH + 2 * PAD, LANE), F32)

    pl.when(has_right)(to_left[3].wait_recv)
    pl.when(has_left)(to_right[3].wait_recv)
    for first in (TOP, UPPER, LOWER, BOTTOM):
        compute(first, OUTER)
    send(7)
    send(8)

    for there, ref in ((has_next, next_ref), (has_prev, prev_ref)):
        @pl.when(jnp.logical_not(there))
        def _(ref=ref):
            ref[...] = jnp.zeros((TH, TW), F32)

    for g, (group, (blocks, rows)) in enumerate(zip(GROUPS, ARRIVALS)):
        region = (pl.ds(0, blocks), pl.ds(0, rows))

        @pl.when(has_next)
        def _(g=g, group=group, region=region):
            transfer(0, g, region).wait_recv()
            for first, rows, left, blocks in group:
                for j in range(left, left + blocks):
                    where = (j, slice(first, first + rows))
                    next_ref[first:first + rows, j * LANE:(j + 1) * LANE] = bn[where] - dog[where]

        @pl.when(has_prev)
        def _(g=g, group=group, region=region):
            transfer(1, g, region).wait_recv()
            for first, rows, left, blocks in group:
                for j in range(left, left + blocks):
                    where = (j, slice(first, first + rows))
                    prev_ref[first:first + rows, j * LANE:(j + 1) * LANE] = dog[where] - bp[where]

    tile = (pl.ds(0, TW // LANE), pl.ds(0, TH))
    pl.when(has_prev)(transfer(0, 0, tile).wait_send)
    pl.when(has_next)(transfer(1, 0, tile).wait_send)
    pl.when(has_above)(to_above.wait_send)
    pl.when(has_below)(to_below.wait_send)
    pl.when(has_left)(to_left[3].wait_send)
    pl.when(has_right)(to_right[3].wait_send)


def flush(next_in, prev_in, next_out, prev_out, sem):
    copies = [pltpu.make_async_copy(next_in, next_out, sem.at[0]), pltpu.make_async_copy(prev_in, prev_out, sem.at[1])]
    for copy in copies:
        copy.start()
    for copy in copies:
        copy.wait()


def body(raster, shift_pick, offsets):
    tile = jax.ShapeDtypeStruct((TH, TW), F32)
    wide, high = TW + 2 * LANE, TH + 2 * PAD
    dma = pltpu.SemaphoreType.DMA
    next_map, prev_map = pl.pallas_call(
        kernel,
        out_shape=[tile, tile],
        in_specs=[pl.BlockSpec(memory_space=pltpu.SMEM)] + [pl.BlockSpec(memory_space=pltpu.HBM)] * 2,
        out_specs=[pl.BlockSpec(memory_space=pltpu.VMEM)] * 2,
        scratch_shapes=[
            pltpu.SMEM((1, 1, 1, 2), jnp.int32),
            pltpu.VMEM((high, wide), F32),
            pltpu.VMEM((3 * LANE, 2 * LANE), BF16), pltpu.VMEM((3 * LANE, 2 * LANE), BF16),
            pltpu.VMEM((ROWS, 2 * SPAN), BF16), pltpu.VMEM((ROWS, 2 * SPAN), BF16),
            pltpu.VMEM((2 * SPAN, 2 * LANE), BF16), pltpu.VMEM((2 * SPAN, 2 * LANE), BF16),
            *[pltpu.VMEM((TW // LANE, TH, LANE), F32)] * 3,
            dma((3,)), dma((2,)), dma((2,)), dma((2,)), dma((2,)), dma((2,)), dma((2, 3)), pltpu.SemaphoreType.REGULAR((4,)),
        ],
        compiler_params=pltpu.CompilerParams(collective_id=0, has_side_effects=True, vmem_limit_bytes=32 * 1024 * 1024),
    )(shift_pick, *(pltpu.with_memory_space_constraint(x, pltpu.HBM) for x in (offsets, raster[0])))
    maps = pl.pallas_call(
        flush,
        out_shape=[tile, tile],
        in_specs=[pl.BlockSpec(memory_space=pltpu.VMEM)] * 2,
        out_specs=[pl.BlockSpec(memory_space=pltpu.HBM)] * 2,
        scratch_shapes=[dma((2,))],
        compiler_params=pltpu.CompilerParams(vmem_limit_bytes=4 * 1024 * 1024),
    )(*(pltpu.with_memory_space_constraint(x, pltpu.VMEM) for x in (next_map, prev_map)))
    return maps[0][None], maps[1][None]


def solution(mesh):
    in_specs = (P("die", "ty", "tx"), P("die", "ty", "tx"), P("die", "ty", "tx", None))
    out_specs = (P("die", "ty", "tx"), P("die", "ty", "tx"))
    return jax.shard_map(body, mesh=mesh, in_specs=in_specs, out_specs=out_specs, check_vma=False)
```

```python
import functools
import math

import jax
import jax.numpy as jnp
from jax import lax
from jax.experimental import pallas as pl
from jax.experimental.pallas import tpu as pltpu
from jax.sharding import PartitionSpec as P

MESH = pl.DeviceIdType.MESH
F32, BF16 = jnp.float32, jnp.bfloat16
TH, TW = 256, 1024
RG = 6
PAD = 16
LANE = 128
ROWS = 64
SPAN = ROWS + 2 * PAD
UPPER, LOWER, TOP, BOTTOM = 64, 128, 0, 192
INNER = ((1, 2), (3, 4), (5, 6))
OUTER = (0, 7)
GROUPS = (((64, 64, 1, 1), (64, 64, 2, 1), (128, 64, 1, 2), (64, 128, 3, 2), (64, 128, 5, 2)),
          ((0, 64, 1, 6), (192, 64, 1, 6)),
          ((0, 256, 0, 1), (0, 256, 7, 1)))
ARRIVALS = ((128, 768), (128, 768), (256, 256))


def start_rank(die, ty, tx):
    late_first = jnp.where((die == 0) & (ty == 0) & (tx == 0), 50, 0)
    return 13 * ty + 50 * lax.div(tx, 2) - 4 * lax.rem(tx, 2) + late_first


def tap_weights(step, sigma, frac):
    norm = sum(math.exp(-k * k / (2.0 * sigma * sigma)) for k in range(-RG, RG + 1))

    def gauss(k):
        spot = k.astype(F32)
        value = jnp.exp(spot * spot * (-1.0 / (2.0 * sigma * sigma))) * (1.0 / norm)
        return jnp.where(jnp.abs(k) <= RG, value, 0.0)

    return (1.0 - frac) * gauss(step) + frac * gauss(step - 1)


def split(x):
    high = x.astype(BF16)
    return high, (x - high.astype(F32)).astype(BF16)


def product(ah, al, bh, bl):
    dot = functools.partial(jnp.dot, preferred_element_type=F32)
    return dot(ah, bh) + dot(ah, bl) + dot(al, bh)


def kernel(pick_ref, off_hbm, x_ref, next_ref, prev_ref, off_ref, pf, wh, wl, yh, yl, hh, hl, dog, bn, bp,
           load_sem, row_send, row_recv, col_send, col_recv, send_sem, recv_sem, ready):
    die, ty, tx = lax.axis_index("die"), lax.axis_index("ty"), lax.axis_index("tx")
    dies, tys, txs = lax.axis_size("die"), lax.axis_size("ty"), lax.axis_size("tx")
    has_next, has_prev = die < dies - 1, die > 0
    bar = pltpu.get_barrier_semaphore()
    for flag, target in ((has_next, die + 1), (has_prev, die - 1)):
        @pl.when(flag)
        def _(target=target):
            pl.semaphore_signal(bar, inc=1, device_id={"die": target}, device_id_type=MESH)

    def load(i, first, rows, left, columns):
        return pltpu.make_async_copy(x_ref.at[pl.ds(first, rows), pl.ds(left, columns)],
                                     pf.at[pl.ds(PAD + first, rows), pl.ds(LANE + left, columns)], load_sem.at[i])

    small = pltpu.make_async_copy(off_hbm, off_ref, load_sem.at[0])
    loads = (load(1, 48, 96, 0, 512), load(2, 144, 64, 0, 512), load(3, 48, 160, 512, 512), load(4, 0, 96, 0, TW))
    small.start()
    for first in (48, 80, 112):
        load(1, first, 32, 0, 512).start()
    for copy in (loads[1], loads[2], load(4, 0, 48, 0, TW), load(4, 208, 48, 0, TW)):
        copy.start()

    has_above, has_below, has_left, has_right = ty > 0, ty < tys - 1, tx > 0, tx < txs - 1
    count = lambda flags: sum(flag.astype(jnp.int32) for flag in flags)

    here = start_rank(die, ty, tx)
    sides = (({"ty": ty + 1}, has_below, (die, ty + 1, tx), 1), ({"ty": ty - 1}, has_above, (die, ty - 1, tx), 0),
             ({"tx": tx + 1}, has_right, (die, ty, tx + 1), 3), ({"tx": tx - 1}, has_left, (die, ty, tx - 1), 2))
    follows = [there & (start_rank(*spot) > here) for _, there, spot, _ in sides]
    leads = [there & (start_rank(*spot) < here) for _, there, spot, _ in sides]
    BELOW, ABOVE, RIGHT, LEFT = range(4)

    def await_follower(side):
        pl.when(follows[side])(lambda: pl.semaphore_wait(ready.at[side], 1))

    for (target, _, _, _), flag in zip(sides, follows):
        @pl.when(flag)
        def _(target=target):
            pl.semaphore_signal(bar, inc=1, device_id=target, device_id_type=MESH)

    band = slice(LANE - PAD, 2 * LANE + PAD)
    for w in (wh, wl):
        w[0:LANE - PAD, :] = jnp.zeros((LANE - PAD, 2 * LANE), BF16)
        w[2 * LANE + PAD:, :] = jnp.zeros((LANE - PAD, 2 * LANE), BF16)
    pick = pick_ref[0, 0, 0]
    frac_y = lax.rem(pick, 4).astype(F32) * 0.25 + 0.125
    frac_x = lax.div(pick, 4).astype(F32) * 0.5 + 0.25
    small.wait()
    row_off, col_off = off_ref[0, 0, 0, 0], off_ref[0, 0, 0, 1]
    iota = lambda shape, dim: lax.broadcasted_iota(jnp.int32, shape, dim)
    step = iota((LANE + 2 * PAD, LANE), 0) - PAD - iota((LANE + 2 * PAD, LANE), 1) - col_off
    for s, sigma in enumerate((1.0, 2.0)):
        lanes = slice(s * LANE, (s + 1) * LANE)
        wh[band, lanes], wl[band, lanes] = split(tap_weights(step, sigma, frac_x))
    column = iota((ROWS, 2 * SPAN), 1)
    step = jnp.where(column < SPAN, column, column - SPAN) - PAD - iota((ROWS, 2 * SPAN), 0) - row_off
    yh[...], yl[...] = split(jnp.where(column < SPAN, tap_weights(step, 1.0, frac_y), -tap_weights(step, 2.0, frac_y)))

    def compute(first, pair):
        level = jnp.mean(pf[first + 40:first + 48, (pair[0] + 1) * LANE:(pair[0] + 2) * LANE], keepdims=True)
        for n, j in enumerate(pair):
            if pair == OUTER and n == 1:
                level = jnp.mean(pf[first + 40:first + 48, (j + 1) * LANE:(j + 2) * LANE], keepdims=True)
            high, low = split(product(*split(pf[first:first + SPAN, j * LANE:(j + 3) * LANE] - level), wh[...], wl[...]))
            for s in range(2):
                where = (slice(s * SPAN, (s + 1) * SPAN), slice(n * LANE, (n + 1) * LANE))
                hh[where], hl[where] = high[:, s * LANE:(s + 1) * LANE], low[:, s * LANE:(s + 1) * LANE]
        wide = slice(0, len(pair) * LANE)
        d = product(yh[...], yl[...], hh[:, wide], hl[:, wide])
        for n, j in enumerate(pair):
            dog[first:first + ROWS, j * LANE:(j + 1) * LANE] = d[:, n * LANE:(n + 1) * LANE]

    def transfer(k, group, where):
        target, landing = ((die - 1, bn), (die + 1, bp))[k]
        return pltpu.make_async_remote_copy(src_ref=dog.at[where], dst_ref=landing.at[where], send_sem=send_sem.at[k], recv_sem=recv_sem.at[k, group],
                                            device_id={"die": target}, device_id_type=MESH)

    spots = [[(pl.ds(first, rows), pl.ds(left * LANE, blocks * LANE)) for first, rows, left, blocks in group] for group in GROUPS]
    pieces = [[transfer(k, g, where) for k in range(2)] for g, group in enumerate(spots) for where in group]

    def send(i):
        to_prev, to_next = pieces[i]
        pl.when(has_prev)(to_prev.start)
        pl.when(has_next)(to_next.start)

    core = pl.ds(LANE, TW)
    to_above, to_below = (
        pltpu.make_async_remote_copy(src_ref=pf.at[pl.ds(source, PAD), core], dst_ref=pf.at[pl.ds(target, PAD), core], send_sem=row_send.at[i],
                                     recv_sem=row_recv.at[i], device_id={"ty": to}, device_id_type=MESH)
        for i, (source, target, to) in enumerate(((PAD, PAD + TH, ty - 1), (TH, 0, ty + 1))))
    parts = (pl.ds(PAD, TH), pl.ds(0, PAD), pl.ds(PAD + TH, PAD), pl.ds(0, TH + 2 * PAD))
    to_left, to_right = (
        [pltpu.make_async_remote_copy(src_ref=pf.at[rows, pl.ds(source, LANE)], dst_ref=pf.at[rows, pl.ds(target, LANE)], send_sem=col_send.at[i],
                                      recv_sem=col_recv.at[i], device_id={"tx": to}, device_id_type=MESH) for rows in parts]
        for i, (source, target, to) in enumerate(((LANE, LANE + TW, tx - 1), (TW, 0, tx + 1))))

    loads[0].wait()
    compute(UPPER, INNER[0][:1])
    pl.semaphore_wait(bar, count([has_next, has_prev] + leads))
    for (target, _, _, slot), flag in zip(sides, leads):
        @pl.when(flag)
        def _(target=target, slot=slot):
            pl.semaphore_signal(ready.at[slot], inc=1, device_id=target, device_id_type=MESH)

    send(0)
    compute(UPPER, INNER[0][1:])
    send(1)
    loads[1].wait()
    compute(LOWER, INNER[0])
    send(2)
    loads[2].wait()
    loads[3].wait()
    pl.when(leads[ABOVE])(to_above.start)
    pl.when(leads[BELOW])(to_below.start)
    pl.when(leads[LEFT])(to_left[0].start)
    pl.when(leads[RIGHT])(to_right[0].start)
    for i, pair in enumerate(INNER[1:]):
        compute(UPPER, pair)
        compute(LOWER, pair)
        send(3 + i)
    for side, copy in ((BELOW, to_below), (ABOVE, to_above)):
        await_follower(side)
        pl.when(follows[side])(copy.start)

    @pl.when(ty == 0)
    def _():
        pf[0:PAD, LANE:LANE + TW] = jnp.zeros((PAD, TW), F32)

    @pl.when(ty == tys - 1)
    def _():
        pf[PAD + TH:, LANE:LANE + TW] = jnp.zeros((PAD, TW), F32)

    pl.when(has_below)(to_above.wait_recv)
    pl.when(has_above)(to_below.wait_recv)
    for i in (1, 2):
        pl.when(leads[LEFT])(to_left[i].start)
        pl.when(leads[RIGHT])(to_right[i].start)
    for i, first in enumerate((TOP, BOTTOM)):
        for pair in INNER:
            compute(first, pair)
        send(5 + i)

    for side, copies in ((RIGHT, to_right), (LEFT, to_left)):
        await_follower(side)
        for copy in copies[:3]:
            pl.when(follows[side])(copy.start)

    @pl.when(tx == 0)
    def _():
        pf[:, 0:LANE] = jnp.zeros((TH + 2 * PAD, LANE), F32)

    @pl.when(tx == txs - 1)
    def _():
        pf[:, LANE + TW:] = jnp.zeros((TH + 2 * PAD, LANE), F32)

    pl.when(has_right)(to_left[3].wait_recv)
    pl.when(has_left)(to_right[3].wait_recv)
    for first in (TOP, UPPER, LOWER, BOTTOM):
        compute(first, OUTER)

    for there, ref in ((has_next, next_ref), (has_prev, prev_ref)):
        @pl.when(jnp.logical_not(there))
        def _(ref=ref):
            ref[...] = jnp.zeros((TH, TW), F32)

    for g, (group, (rows, columns)) in enumerate(zip(spots, ARRIVALS)):
        block = (pl.ds(0, rows), pl.ds(0, columns))

        @pl.when(has_next)
        def _(g=g, group=group, block=block):
            transfer(0, g, block).wait_recv()
            for where in group:
                next_ref[where] = bn[where] - dog[where]

        @pl.when(has_prev)
        def _(g=g, group=group, block=block):
            transfer(1, g, block).wait_recv()
            for where in group:
                prev_ref[where] = dog[where] - bp[where]

        if g == 0:
            send(7)
            send(8)

    tile = (pl.ds(0, TH), pl.ds(0, TW))
    pl.when(has_prev)(transfer(0, 0, tile).wait_send)
    pl.when(has_next)(transfer(1, 0, tile).wait_send)
    pl.when(has_above)(to_above.wait_send)
    pl.when(has_below)(to_below.wait_send)
    pl.when(has_left)(to_left[3].wait_send)
    pl.when(has_right)(to_right[3].wait_send)


def flush(next_in, prev_in, next_out, prev_out, sem):
    copies = [pltpu.make_async_copy(next_in, next_out, sem.at[0]), pltpu.make_async_copy(prev_in, prev_out, sem.at[1])]
    for copy in copies:
        copy.start()
    for copy in copies:
        copy.wait()


def body(raster, shift_pick, offsets):
    tile = jax.ShapeDtypeStruct((TH, TW), F32)
    wide, high = TW + 2 * LANE, TH + 2 * PAD
    dma = pltpu.SemaphoreType.DMA
    next_map, prev_map = pl.pallas_call(
        kernel,
        out_shape=[tile, tile],
        in_specs=[pl.BlockSpec(memory_space=pltpu.SMEM)] + [pl.BlockSpec(memory_space=pltpu.HBM)] * 2,
        out_specs=[pl.BlockSpec(memory_space=pltpu.VMEM)] * 2,
        scratch_shapes=[
            pltpu.SMEM((1, 1, 1, 2), jnp.int32),
            pltpu.VMEM((high, wide), F32),
            pltpu.VMEM((3 * LANE, 2 * LANE), BF16), pltpu.VMEM((3 * LANE, 2 * LANE), BF16),
            pltpu.VMEM((ROWS, 2 * SPAN), BF16), pltpu.VMEM((ROWS, 2 * SPAN), BF16),
            pltpu.VMEM((2 * SPAN, 2 * LANE), BF16), pltpu.VMEM((2 * SPAN, 2 * LANE), BF16),
            pltpu.VMEM((TH, TW), F32), pltpu.VMEM((TH, TW), F32), pltpu.VMEM((TH, TW), F32),
            dma((5,)), dma((2,)), dma((2,)), dma((2,)), dma((2,)), dma((2,)), dma((2, 3)), pltpu.SemaphoreType.REGULAR((4,)),
        ],
        compiler_params=pltpu.CompilerParams(collective_id=0, has_side_effects=True, vmem_limit_bytes=32 * 1024 * 1024),
    )(shift_pick, *(pltpu.with_memory_space_constraint(x, pltpu.HBM) for x in (offsets, raster[0])))
    maps = pl.pallas_call(
        flush,
        out_shape=[tile, tile],
        in_specs=[pl.BlockSpec(memory_space=pltpu.VMEM)] * 2,
        out_specs=[pl.BlockSpec(memory_space=pltpu.HBM)] * 2,
        scratch_shapes=[dma((2,))],
        compiler_params=pltpu.CompilerParams(vmem_limit_bytes=4 * 1024 * 1024),
    )(*(pltpu.with_memory_space_constraint(x, pltpu.VMEM) for x in (next_map, prev_map)))
    return maps[0][None], maps[1][None]


def solution(mesh):
    in_specs = (P("die", "ty", "tx"), P("die", "ty", "tx"), P("die", "ty", "tx", None))
    out_specs = (P("die", "ty", "tx"), P("die", "ty", "tx"))
    return jax.shard_map(body, mesh=mesh, in_specs=in_specs, out_specs=out_specs, check_vma=False)
```
